32 devices in a mesh: dp: 8 (over y, x, core), shard: 4 (over z).
Axes of the slice: x: 2, y: 2, z: 4, core: 2. Of those that a mesh axis runs over, the one named last changes fastest.
Arguments:
- activations: bfloat16 [4096, 4096], P('dp', 'shard'), may hold values from -6 to 6
- out_grads: bfloat16 [4096, 14336], P('dp', 'shard'), may hold values from -6 to 6
- sign_bits: int32 [14336], P('shard'), may hold values from 0 to 1
- block_ids: int32 [4, 8], replicated, may hold values from 0 to 111, as said below
Outputs:
- gram: float32 [4096, 1024], P('shard')
The draws below stay inside these ranges and needn't reach their ends.
Inputs may be any that keep to these rules, and one draw needn't show every extreme that they name: `block_ids`: row o holds 4 runs of 2 entries; the entries of a run are distinct blocks of one shard s (ids s * 28 + 0 to s * 28 + 27), and the runs of a row come from distinct shards.
All inputs are finite; a program needn't handle non-finite values.
Results may differ from the reference program's by a relative error of at most 0.006.
Values may be sent and summed in bfloat16 or wider, within the bound.
A program may use at most 64 MiB of HBM per device.

```python
import math
import jax
import jax.numpy as jnp
from jax import lax

D = 4096
FF = 14336
BLK = 128
CAP = 2
GROUPS = 4
TOK = 512
BPS = 28
NBLK = 112
OWN_BLOCKS = 8
OWN = 1024
ROWS = 4096
N_DP = 8
N_SHARD = 4


def draw_block_ids(key, part):
    key_hot, key_pick, key_order = jax.random.split(key, 3)
    hot_shards = jax.random.randint(key_hot, (N_SHARD,), 0, 2)
    pick_noise = jax.random.randint(key_pick, (N_SHARD, N_SHARD), 0, 8)
    shard_scores = (pick_noise + 4 * hot_shards[None, :]) * N_SHARD + jnp.arange(N_SHARD, dtype=jnp.int32)[None, :]
    unused, sources = lax.top_k(shard_scores, GROUPS)
    order_scores = jax.random.randint(key_order, (N_SHARD, GROUPS, BPS), 0, 1 << 20) * BPS + jnp.arange(BPS, dtype=jnp.int32)
    local_ids = jnp.argsort(order_scores, axis=-1)[:, :, :CAP]
    return (sources[:, :, None] * BPS + local_ids).reshape(N_SHARD, GROUPS * CAP).astype(jnp.int32)


def plant(entries, key, low, high):
    longest = entries.shape.index(max(entries.shape))
    spots = []
    for shift in (0, 1):
        where = [jax.random.randint(jax.random.fold_in(key, axis), (), 0, length) for axis, length in enumerate(entries.shape)]
        where[longest] = (where[longest] + shift) % entries.shape[longest]
        spots.append(tuple(where))
    return entries.at[spots[0]].set(low).at[spots[1]].set(high)


def block_levels(key, dims, cuts, low, largest):
    level, own = 1.0, jax.random.fold_in(key, 6)
    for dim, parts in cuts:
        steps = jnp.exp(jax.random.uniform(jax.random.fold_in(own, dim), (parts,), jnp.float32, low / len(cuts), largest / len(cuts)))
        level = level * jnp.repeat(steps, dims[dim] // parts).reshape([-1 if axis == dim else 1 for axis in range(len(dims))])
    return level


def gaussian(key, dims, scale, most, shards=(), kind=jnp.bfloat16):
    values = scale * jax.random.normal(key, dims, jnp.float32)
    if shards:
        values = values * block_levels(key, dims, shards, -0.22, 0.18)
    return jnp.clip(values, -most, most).astype(kind)


def setup_inputs(seed: int = 0) -> dict:
    splits = jax.random.split(jax.random.key(seed), 5)
    return {
        "activations": gaussian(splits[0], (ROWS, D), 1.0, 6.0, ((0, 8), (1, 4))),
        "out_grads": gaussian(splits[1], (ROWS, FF), 1.0, 6.0, ((0, 8), (1, 4))),
        "sign_bits": plant(jax.random.randint(splits[2], (FF,), 0, 2), jax.random.fold_in(splits[2], 1), 0, 1).astype(jnp.int32),
        "block_ids": draw_block_ids(jax.random.fold_in(splits[4], 71), 0),
    }


def parity_table(count):
    index = jnp.arange(count, dtype=jnp.int32)
    total = jnp.zeros((count, count), jnp.int32)
    for level in range(count.bit_length() - 1):
        total = total + (jnp.right_shift(index[:, None], level) & jnp.right_shift(index[None, :], level) & 1)
    return (1 - 2 * (total % 2)).astype(jnp.float32)

def reference(activations, out_grads, sign_bits, block_ids):
    highest = lax.Precision.HIGHEST
    block_table = parity_table(BLK)
    shard_table = parity_table(N_SHARD)
    sign_values = (1 - 2 * sign_bits).astype(jnp.bfloat16)
    seq_acts = activations.reshape(N_DP, TOK, D)
    seq_grads = out_grads.reshape(N_DP, TOK, FF)

    def accumulate(running, example_pair):
        example_acts, example_grads = example_pair
        token_gram = jnp.dot(example_acts, example_acts.T, preferred_element_type=jnp.float32).astype(jnp.bfloat16)
        flipped = (example_grads * sign_values[None, :]).reshape(TOK, N_SHARD, BPS, BLK)
        local_mix = jnp.einsum('tsbj,jk->tsbk', flipped.astype(jnp.float32), block_table, precision=highest)
        local_mix = (local_mix * (1.0 / math.sqrt(BLK))).astype(jnp.bfloat16)
        mixed = jnp.einsum('rs,tsbk->rbtk', shard_table, local_mix.astype(jnp.float32), precision=highest)
        mixed = (mixed * (1.0 / math.sqrt(N_SHARD))).astype(jnp.bfloat16).reshape(NBLK, TOK, BLK)
        sketched = jnp.take(mixed, block_ids.reshape(-1), axis=0).reshape(N_SHARD, OWN_BLOCKS, TOK, BLK)
        weighted = jnp.einsum('tu,ojub->ojtb', token_gram.astype(jnp.float32), sketched.astype(jnp.float32), precision=highest).astype(jnp.bfloat16)
        block_gram = jnp.einsum('ojtb,oktc->ojbkc', sketched.astype(jnp.float32), weighted.astype(jnp.float32), precision=highest)
        return (running + block_gram.reshape(N_SHARD * OWN, OWN), None)
    total, unused = lax.scan(accumulate, jnp.zeros((N_SHARD * OWN, OWN), jnp.float32), (seq_acts, seq_grads))
    return total / (N_DP * TOK * D)
```

```python
import functools
import math

import jax
import jax.numpy as jnp
from jax import lax
from jax.experimental import pallas as pl
from jax.experimental.pallas import tpu as pltpu
from jax.sharding import PartitionSpec as P

BLK = 128
CAP = 2


def partner_2(x, axis, distance):
    return lax.ppermute(x, axis, [(i, i ^ 1 << distance) for i in range(lax.axis_size(axis))])


def parity_table(count):
    index = jnp.arange(count, dtype=jnp.int32)
    total = jnp.zeros((count, count), jnp.int32)
    for level in range(count.bit_length() - 1):
        total = total + (
            jnp.right_shift(index[:, None], level) & jnp.right_shift(index[None, :], level) & 1
        )
    return (1 - 2 * (total % 2)).astype(jnp.float32)


def route_sampled(mixed, block_ids, me_index, shards, blocks_per, tokens, width):
    groups = block_ids.shape[1] // CAP
    sources = block_ids[:, ::CAP] // blocks_per
    local_ids = (block_ids % blocks_per).reshape(shards, groups, CAP)
    matched = sources == me_index
    chosen = jnp.sum(jnp.where(matched[:, :, None], local_ids, 0), axis=1)
    live_rows = jnp.any(matched, axis=1).astype(jnp.bfloat16)
    outgoing = jnp.take(mixed, chosen.reshape(-1), axis=0).reshape(shards, CAP, tokens, width)
    return (outgoing * live_rows[:, None, None, None], jnp.take(sources, me_index, axis=0))


def body(activations, out_grads, sign_bits, block_ids):
    shards = lax.axis_size("shard")
    me_index = lax.axis_index("shard")
    tokens = out_grads.shape[0]
    width = BLK
    own_blocks = block_ids.shape[1]
    blocks_per = out_grads.shape[1] // width
    model_width = activations.shape[1] * shards
    inv_block = 1.0 / math.sqrt(width)
    inv_shard = 1.0 / math.sqrt(shards)
    partial_gram = jnp.dot(activations, activations.T, preferred_element_type=jnp.float32)
    token_gram = lax.psum(partial_gram, "shard").astype(jnp.bfloat16)
    sign_values = (1 - 2 * sign_bits).astype(jnp.bfloat16)
    flipped = (out_grads * sign_values[None, :]).reshape(tokens, blocks_per, width)
    block_table = parity_table(width).astype(jnp.bfloat16)
    local_mix = jnp.einsum("tbj,jk->btk", flipped, block_table, preferred_element_type=jnp.float32)
    local_mix = (local_mix * inv_block).astype(jnp.bfloat16)
    running = local_mix.astype(jnp.float32)
    for level in range(shards.bit_length() - 1):
        partner = partner_2(running, "shard", level)
        upper = jnp.right_shift(me_index, level) & 1 == 1
        running = jnp.where(upper, partner - running, running + partner)
    mixed = (running * inv_shard).astype(jnp.bfloat16)
    outgoing, own_sources = route_sampled(
        mixed, block_ids, me_index, shards, blocks_per, tokens, width
    )
    incoming = lax.all_to_all(outgoing, "shard", split_axis=0, concat_axis=0, tiled=True)
    sketched = jnp.take(incoming, own_sources, axis=0).reshape(own_blocks, tokens, width)
    weighted = jnp.einsum(
        "tu,jub->jtb", token_gram, sketched, preferred_element_type=jnp.float32
    ).astype(jnp.bfloat16)
    block_gram = jnp.einsum("jtb,ktc->jbkc", sketched, weighted, preferred_element_type=jnp.float32)
    own_cols = own_blocks * width
    block_gram = block_gram.reshape(own_cols, own_cols)
    summed = lax.psum(block_gram, "dp")
    return summed / (lax.axis_size("dp") * tokens * model_width)


ALONG = pl.DeviceIdType.MESH
COUNT = 8
PIECES = 2 * COUNT
CUTS = 4
GB = 10
TRIANGLE = tuple((i, j) for i in range(4) for j in range(i + 1))
UNITS = COUNT * (COUNT + 1) // 2
ORDER = tuple((1, COUNT - 1) if k == PIECES - 1 else (0, (k + 1) // 2) if k % 2 or k == 0 else (1, k // 2 - 1) for k in range(PIECES))
WHOLE = tuple((j, 0, BLK) for j in range(COUNT))
SPLIT = WHOLE[:-1] + ((COUNT - 1, 0, BLK // 2), (COUNT - 1, BLK // 2, BLK))
CHUNKS = (WHOLE, SPLIT)
STEPS = tuple((t, c, k) for k, (t, j) in enumerate(ORDER) for c, chunk in enumerate(CHUNKS[t]) if chunk[0] == j)


def units_of(chunk):
    j, lo, hi = chunk
    first = j * (j + 1) // 2
    if j < COUNT - 1:
        return first, j + 1
    half = COUNT // 2
    return first + half * (lo // (BLK // 2)), half * ((hi - lo) // (BLK // 2))


def mix_kernel(
    shards, parts, own, per, act_hbm, grads_hbm, bits_hbm, ids_hbm, gathered,
    act, grads, bits, flips, ids, rx, tx, grx, gtx, part, full, sketch, keep, give, prx, rtx, rrx,
    l_sem, z_send, z_recv, p_send, p_recv, r_send, r_recv, f_send, f_recv, a_send, a_recv, w_send, w_recv,
):
    z = lax.axis_index("shard")
    d = lax.axis_index("dp")
    core = lax.rem(d, 2)
    chip = d // 2
    last = shards - 1
    edge = (z == 0) | (z == last)
    middle = jnp.logical_not(edge)
    tokens = act.shape[0]
    width = BLK
    inv_block = 1.0 / math.sqrt(width)
    inv_shard = 1.0 / math.sqrt(shards)
    quarter = width // CUTS

    barrier = pltpu.get_barrier_semaphore()

    def peer(m):
        flipped = 1 - lax.rem(chip, 2) if m & 1 else lax.rem(chip, 2)
        high = 1 - chip // 2 if m & 2 else chip // 2
        return (high * 2 + flipped) * 2 + core

    partner = chip * 2 + 1 - core
    for m in (1, 2, 3):
        pl.semaphore_signal(barrier, inc=1, device_id={"dp": peer(m)}, device_id_type=ALONG)
    pl.semaphore_signal(barrier, inc=1, device_id={"dp": partner}, device_id_type=ALONG)

    @pl.when(z > 0)
    def _():
        pl.semaphore_signal(barrier, inc=1, device_id={"shard": z - 1}, device_id_type=ALONG)

    @pl.when(z < last)
    def _():
        pl.semaphore_signal(barrier, inc=1, device_id={"shard": z + 1}, device_id_type=ALONG)

    loads = (
        pltpu.make_async_copy(act_hbm, act, l_sem.at[0]),
        pltpu.make_async_copy(ids_hbm, ids, l_sem.at[1]),
        pltpu.make_async_copy(bits_hbm, bits, l_sem.at[2]),
    ) + tuple(
        pltpu.make_async_copy(grads_hbm.at[:, pl.ds(width * b, width)], grads.at[b], l_sem.at[3 + b]) for b in range(per)
    )
    for load in loads:
        load.start()

    row = lax.broadcasted_iota(jnp.int32, (width, width), 0)
    col = lax.broadcasted_iota(jnp.int32, (width, width), 1)
    both = row & col
    count = both & 1
    for level in range(1, width.bit_length() - 1):
        count = count + ((both >> level) & 1)
    table = (1 - 2 * (count & 1)).astype(jnp.float32)

    def contribution(owner, j):
        block = ids[owner, j]
        r = lax.div(block, per)
        local = block - r * per
        common = r & z
        odd = common & 1
        for level in range(1, shards.bit_length() - 1):
            odd = odd + ((common >> level) & 1)
        sign = 1 - 2 * (odd & 1)
        signs = flips[local] * sign.astype(jnp.float32)
        lm = lax.dot_general(
            (table * signs).astype(jnp.bfloat16), grads[local], (((1,), (1,)), ((), ())),
            preferred_element_type=jnp.float32)
        return ((lm * inv_block).astype(jnp.bfloat16).astype(jnp.float32) * inv_shard).astype(jnp.bfloat16)

    def owner_of(way, t):
        return jnp.where(way == 0, 1 - t, 2 + t)

    def piece(k):
        if isinstance(k, int):
            return ORDER[k]
        odd = lax.rem(k, 2) == 1
        final = k == PIECES - 1
        t = jnp.where(final | jnp.logical_not(odd | (k == 0)), 1, 0)
        j = jnp.where(final, COUNT - 1, jnp.where(t == 1, k // 2 - 1, (k + 1) // 2))
        return t, j

    def target(way):
        return jnp.where(way == 0, z - 1, z + 1)

    def s_move(way, k, h, who):
        rows = pl.ds(quarter * h, quarter)
        n = GB + CUTS * k + h
        return pltpu.make_async_remote_copy(
            tx.at[way, k, rows], rx.at[way, k, rows], z_send.at[way, n], z_recv.at[way, n],
            device_id={"shard": who}, device_id_type=ALONG)

    def s_copy(way, k, h):
        return s_move(way, k, h, target(way))

    def g_move(way, n, who):
        return pltpu.make_async_remote_copy(
            gtx.at[way, n], grx.at[way, n], z_send.at[way, n], z_recv.at[way, n],
            device_id={"shard": who}, device_id_type=ALONG)

    def g_copy(way, n):
        return g_move(way, n, target(way))

    def gpart(n):
        i, j = TRIANGLE[n]
        return part[128 * i : 128 * (i + 1), 128 * j : 128 * (j + 1)]

    def fill(way, k):
        t, j = piece(k)
        tx[way, k] = contribution(owner_of(way, t), j)

    def units(t, c):
        return pl.ds(*units_of(CHUNKS[t][c]))

    def a_move(t, c, slot, who, holder):
        return pltpu.make_async_remote_copy(
            gathered.at[holder, units(t, c)], gathered.at[holder, units(t, c)], a_send.at[c, slot], a_recv.at[c, slot],
            device_id={"dp": who}, device_id_type=ALONG)

    def w_move(t, c, m, holder):
        return pltpu.make_async_remote_copy(
            gathered.at[holder, units(t, c)], gathered.at[holder, units(t, c)],
            w_send.at[c, m - 1], w_recv.at[c, m - 1],
            device_id={"dp": partner}, device_id_type=ALONG)

    def spread(t, c):
        for m in (1, 2, 3):
            a_move(t, c, m - 1, peer(m), d).start()
        a_move(t, c, 3, partner, d).start()

    def relay(t, c):
        for m in (1, 2, 3):
            a_move(t, c, m - 1, peer(m), peer(m)).wait_recv()
            w_move(t, c, m, peer(m)).start()

    def settle(t, c):
        a_move(t, c, 3, partner, partner).wait_recv()
        for m in (1, 2, 3):
            w_move(t, c, m, peer(m) + 1 - 2 * core).wait_recv()
        for m in (1, 2, 3):
            a_move(t, c, m - 1, peer(m), d).wait_send()
            w_move(t, c, m, peer(m)).wait_send()
        a_move(t, c, 3, partner, d).wait_send()

    def f_copy(c, who):
        us = units(0, c)
        return pltpu.make_async_remote_copy(
            rrx.at[3, us], gathered.at[d, us], f_send.at[c], f_recv.at[c],
            device_id={"shard": who}, device_id_type=ALONG)

    loads[0].wait()
    part[...] = lax.dot_general(act[...], act[...], (((1,), (1,)), ((), ())), preferred_element_type=jnp.float32)
    for load in loads[1:]:
        load.wait()
    for b in range(per):
        flips[b] = (1 - 2 * bits[width * b : width * (b + 1)].reshape(1, width)).astype(jnp.float32)

    @pl.when(edge)
    def _():
        pl.semaphore_wait(barrier, 5)

    @pl.when(middle)
    def _():
        pl.semaphore_wait(barrier, 6)

    @pl.when(edge)
    def _():
        out_way = jnp.where(z == 0, 1, 0)
        in_way = 1 - out_way
        side = target(out_way)
        for n in range(GB):
            gtx[out_way, n] = gpart(n).astype(jnp.bfloat16)
            g_copy(out_way, n).start()

        def push(k, carry):
            fill(out_way, k)
            for h in range(CUTS):
                s_copy(out_way, k, h).start()
            return carry

        lax.fori_loop(0, PIECES, push, 0)

        def ready(p, carry):
            t, j = p // COUNT, lax.rem(p, COUNT)
            sketch[t, pl.ds(pl.multiple_of(width * j, width), width)] = contribution(owner_of(in_way, t), j)
            return carry

        lax.fori_loop(0, PIECES, ready, 0)

        for n in range(GB):
            g_move(in_way, n, side).wait_recv()
            r, c = TRIANGLE[n]
            block = (grx[in_way, n].astype(jnp.float32) + gpart(n)).astype(jnp.bfloat16)
            full[128 * r : 128 * (r + 1), 128 * c : 128 * (c + 1)] = block
            if r != c:
                full[128 * c : 128 * (c + 1), 128 * r : 128 * (r + 1)] = block.T

        def where(q):
            t, c, k = STEPS[q]
            first, number = units_of(CHUNKS[t][c])
            return t, c, k, pl.ds(UNITS * t + first, number)

        def p_copy(q):
            t, c, k, us = where(q)
            return pltpu.make_async_remote_copy(
                give.at[us], prx.at[us], p_send.at[q], p_recv.at[q],
                device_id={"dp": partner}, device_id_type=ALONG)

        def r_copy(q, m):
            t, c, k, us = where(q)
            return pltpu.make_async_remote_copy(
                rtx.at[peer(m) // 2, us], rrx.at[m - 1, us], r_send.at[q, m - 1], r_recv.at[q, m - 1],
                device_id={"dp": peer(m)}, device_id_type=ALONG)

        def step_a(q):
            t, c, k, us = where(q)
            j, lo, hi = CHUNKS[t][c]
            for h in range(lo // quarter, hi // quarter):
                s_move(in_way, k, h, side).wait_recv()
                rows = slice(width * j + quarter * h, width * j + quarter * (h + 1))
                arrived = rx[in_way, k, quarter * h : quarter * (h + 1)].astype(jnp.float32)
                sketch[t, rows] = (arrived + sketch[t, rows].astype(jnp.float32)).astype(jnp.bfloat16)
            mine = sketch[t, width * j + lo : width * j + hi]
            weighted = jnp.dot(mine, full[...], preferred_element_type=jnp.float32).astype(jnp.bfloat16)
            half = width // 2
            first, number = units_of(CHUNKS[t][c])

            def put(u, top, bottom):
                keep[UNITS * t + u] = jnp.where(core == 0, top, bottom)
                give[UNITS * t + u] = jnp.where(core == 0, bottom, top).astype(jnp.bfloat16)

            for i in range(0, j + 1, 2):
                end = min(i + 2, j + 1)
                block = lax.dot_general(
                    weighted, sketch[t, width * i : width * end], (((1,), (1,)), ((), ())),
                    preferred_element_type=jnp.float32)
                if j < COUNT - 1:
                    for n in range(i, end):
                        cols = slice(width * (n - i), width * (n - i + 1))
                        put(first + n, block[:half, cols], block[half:, cols])
                else:
                    for g in range((hi - lo) // half):
                        rows = slice(half * g, half * (g + 1))
                        put(first + COUNT // 2 * g + i // 2, block[rows, :width], block[rows, width:])
            p_copy(q).start()

        def step_b(q):
            t, c, k, us = where(q)
            p_copy(q).wait_recv()
            total = (keep[us] + prx[us].astype(jnp.float32)).astype(jnp.bfloat16)
            for n in range(4):
                rtx[n, us] = total[:, 16 * n : 16 * (n + 1)]
            for m in (1, 2, 3):
                r_copy(q, m).start()

        def step_c(q):
            t, c, k, us = where(q)
            for m in (1, 2, 3):
                r_copy(q, m).wait_recv()
            total = rtx[chip, us].astype(jnp.float32)
            for m in range(3):
                total = total + rrx[m, us].astype(jnp.float32)
            total = (total * (1.0 / (parts * tokens * act.shape[1] * shards))).astype(jnp.bfloat16)
            if t == 0:
                rrx[3, units(t, c)] = total
                f_copy(c, side).start()
            else:
                gathered[d, units(t, c)] = total
                spread(t, c)

        def step_d(q):
            t, c, k, us = where(q)
            if t == 1:
                relay(t, c)
            p_copy(q).wait_send()
            for m in (1, 2, 3):
                r_copy(q, m).wait_send()

        def drain(k, carry):
            for h in range(CUTS):
                s_copy(out_way, k, h).wait_send()
            return carry

        steps = len(STEPS)
        for q in range(steps - 3):
            step_a(q)
            step_b(q)
            if q >= 2:
                step_c(q - 2)
            if q >= 4:
                step_d(q - 4)
        e = steps - 3
        step_a(e)
        step_c(e - 2)
        step_a(e + 1)
        step_b(e)
        step_a(e + 2)
        step_b(e + 1)
        step_c(e - 1)
        step_b(e + 2)
        step_d(e - 4)
        step_d(e - 3)
        step_d(e - 2)
        step_c(e)
        step_c(e + 1)
        step_c(e + 2)
        for n in range(GB):
            g_copy(out_way, n).wait_send()
        lax.fori_loop(0, PIECES, drain, 0)
        for c in range(len(CHUNKS[1]) - 3):
            settle(1, c)
        step_d(e - 1)
        for c in range(len(CHUNKS[0])):
            f_copy(c, side).wait_send()
        step_d(e)
        step_d(e + 1)
        step_d(e + 2)
        for c in range(len(CHUNKS[1]) - 3, len(CHUNKS[1])):
            settle(1, c)

    @pl.when(middle)
    def _():
        near = jnp.where(z == 1, 1, 0)
        far = 1 - near
        outward = jnp.where(z == 1, 0, last)

        def pass_g(way, n):
            g_copy(way, n).wait_recv()
            gtx[way, n] = (grx[way, n].astype(jnp.float32) + gpart(n)).astype(jnp.bfloat16)
            g_copy(way, n).start()

        def pass_s(way, k, h):
            s_copy(way, k, h).wait_recv()
            rows = slice(quarter * h, quarter * (h + 1))
            tx[way, k, rows] = (rx[way, k, rows].astype(jnp.float32) + tx[way, k, rows].astype(jnp.float32)).astype(jnp.bfloat16)
            s_copy(way, k, h).start()

        lag = CUTS + 1
        for n in range(GB):
            pass_g(near, n)
            if n >= lag:
                pass_g(far, n - lag)
        fill(near, 0)
        for h in range(CUTS):
            pass_s(near, 0, h)
            pass_g(far, GB - lag + h)
        fill(near, 1)
        fill(far, 0)
        pass_s(near, 1, 0)
        pass_g(far, GB - 1)
        for h in range(1, CUTS):
            pass_s(near, 1, h)
            pass_s(far, 0, h - 1)

        def both_ways(k, carry):
            fill(near, k)
            fill(far, k - 1)
            pass_s(near, k, 0)
            pass_s(far, k - 2, CUTS - 1)
            for h in range(1, CUTS):
                pass_s(near, k, h)
                pass_s(far, k - 1, h - 1)
            return carry

        lax.fori_loop(2, PIECES, both_ways, 0)
        fill(far, PIECES - 1)
        pass_s(far, PIECES - 2, CUTS - 1)
        for h in range(CUTS):
            pass_s(far, PIECES - 1, h)

        chunks = len(CHUNKS[0])
        for way in range(2):
            for n in range(GB):
                g_copy(way, n).wait_send()

        def drain(k, carry):
            for h in range(CUTS):
                s_copy(near, k, h).wait_send()
            return carry

        def drain_far(k, carry):
            for h in range(CUTS):
                s_copy(far, k, h).wait_send()
            return carry

        lax.fori_loop(0, PIECES, drain, 0)
        lax.fori_loop(0, PIECES - 2, drain_far, 0)
        for c in range(chunks):
            f_copy(c, outward).wait_recv()
            spread(0, c)
            if c >= 2:
                relay(0, c - 2)
        lax.fori_loop(PIECES - 2, PIECES, drain_far, 0)
        relay(0, chunks - 2)
        for c in range(chunks - 2):
            settle(0, c)
        relay(0, chunks - 1)
        settle(0, chunks - 2)
        settle(0, chunks - 1)


def assemble_kernel(got, out, held, sems):
    half = BLK // 2

    def unit(u):
        rows = [got[2 * n + h, u] for h in range(2) for n in range(4)]
        return jnp.concatenate(rows, axis=0).astype(jnp.float32)

    def put(i):
        rows = pl.ds(BLK * i, BLK)
        return pltpu.make_async_copy(held.at[rows], out.at[rows], sems.at[i])

    final = COUNT - 1
    first = final * COUNT // 2
    lower = {}
    for v in range(COUNT // 2):
        top, bottom = unit(first + v), unit(first + COUNT // 2 + v)
        for g in range(2):
            rows = slice(half * g, half * (g + 1))
            lower[2 * v + g] = jnp.concatenate([top[rows], bottom[rows]], axis=0)
    square = lower[final]
    row = lax.broadcasted_iota(jnp.int32, (BLK, BLK), 0)
    col = lax.broadcasted_iota(jnp.int32, (BLK, BLK), 1)
    lower[final] = jnp.where((row < half) & (col >= half), square.T, square)
    for i in range(COUNT):
        for j in range(COUNT):
            if i == final:
                block = lower[j]
            elif j == final:
                block = lower[i].T
            elif j <= i:
                block = unit(i * (i + 1) // 2 + j)
            else:
                block = unit(j * (j + 1) // 2 + i).T
            held[BLK * i : BLK * (i + 1), BLK * j : BLK * (j + 1)] = block
        put(i).start()
    for i in range(COUNT):
        put(i).wait()


def fast_body(shards, parts, activations, out_grads, sign_bits, block_ids):
    tokens, columns = out_grads.shape
    per = columns // BLK
    own = block_ids.shape[1]
    vmem = pl.BlockSpec(memory_space=pltpu.VMEM)
    hbm = pl.BlockSpec(memory_space=pltpu.HBM)
    bf, f32 = jnp.bfloat16, jnp.float32
    dma = pltpu.SemaphoreType.DMA
    steps, most = len(STEPS), len(CHUNKS[1])
    got = pl.pallas_call(
        functools.partial(mix_kernel, shards, parts, own, per),
        out_shape=jax.ShapeDtypeStruct((parts, UNITS, 16, BLK), bf),
        in_specs=[hbm, hbm, hbm, hbm],
        out_specs=vmem,
        scratch_shapes=[
            pltpu.VMEM(activations.shape, bf),
            pltpu.VMEM((per, tokens, BLK), bf),
            pltpu.VMEM(sign_bits.shape, jnp.int32),
            pltpu.VMEM((per, 1, BLK), f32),
            pltpu.SMEM(block_ids.shape, jnp.int32),
            pltpu.VMEM((2, PIECES, BLK, tokens), bf),
            pltpu.VMEM((2, PIECES, BLK, tokens), bf),
            pltpu.VMEM((2, GB, 128, 128), bf),
            pltpu.VMEM((2, GB, 128, 128), bf),
            pltpu.VMEM((tokens, tokens), f32),
            pltpu.VMEM((tokens, tokens), bf),
            pltpu.VMEM((2, own * BLK, tokens), bf),
            pltpu.VMEM((2 * UNITS, 64, BLK), f32),
            pltpu.VMEM((2 * UNITS, 64, BLK), bf),
            pltpu.VMEM((2 * UNITS, 64, BLK), bf),
            pltpu.VMEM((4, 2 * UNITS, 16, BLK), bf),
            pltpu.VMEM((4, 2 * UNITS, 16, BLK), bf),
            dma((3 + per,)),
            dma((2, GB + CUTS * PIECES)), dma((2, GB + CUTS * PIECES)),
            dma((steps,)), dma((steps,)),
            dma((steps, 3)), dma((steps, 3)),
            dma((COUNT,)), dma((COUNT,)),
            dma((most, 4)), dma((most, 4)),
            dma((most, 3)), dma((most, 3)),
        ],
        compiler_params=pltpu.CompilerParams(collective_id=0, has_side_effects=True, vmem_limit_bytes=40 * 2**20),
        name="mix",
    )(activations, out_grads, sign_bits, block_ids)
    return pl.pallas_call(
        assemble_kernel,
        out_shape=jax.ShapeDtypeStruct((own * BLK, own * BLK), f32),
        in_specs=[vmem],
        out_specs=hbm,
        scratch_shapes=[pltpu.VMEM((own * BLK, own * BLK), f32), dma((own,))],
        compiler_params=pltpu.CompilerParams(vmem_limit_bytes=16 * 2**20),
        name="assemble",
    )(got)


def solution(mesh):
    in_specs = (P("dp", "shard"), P("dp", "shard"), P("shard"), P())
    out_specs = P("shard", None)
    shards, parts = mesh.shape["shard"], mesh.shape["dp"]
    chosen = functools.partial(fast_body, shards, parts) if (shards, parts) == (4, 8) else body
    return jax.shard_map(chosen, mesh=mesh, in_specs=in_specs, out_specs=out_specs, check_vma=False)
```

```python
import functools
import math

import jax
import jax.numpy as jnp
from jax import lax
from jax.experimental import pallas as pl
from jax.experimental.pallas import tpu as pltpu
from jax.sharding import PartitionSpec as P

BLK = 128
CAP = 2


def partner_2(x, axis, distance):
    return lax.ppermute(x, axis, [(i, i ^ 1 << distance) for i in range(lax.axis_size(axis))])


def parity_table(count):
    index = jnp.arange(count, dtype=jnp.int32)
    total = jnp.zeros((count, count), jnp.int32)
    for level in range(count.bit_length() - 1):
        total = total + (
            jnp.right_shift(index[:, None], level) & jnp.right_shift(index[None, :], level) & 1
        )
    return (1 - 2 * (total % 2)).astype(jnp.float32)


def route_sampled(mixed, block_ids, me_index, shards, blocks_per, tokens, width):
    groups = block_ids.shape[1] // CAP
    sources = block_ids[:, ::CAP] // blocks_per
    local_ids = (block_ids % blocks_per).reshape(shards, groups, CAP)
    matched = sources == me_index
    chosen = jnp.sum(jnp.where(matched[:, :, None], local_ids, 0), axis=1)
    live_rows = jnp.any(matched, axis=1).astype(jnp.bfloat16)
    outgoing = jnp.take(mixed, chosen.reshape(-1), axis=0).reshape(shards, CAP, tokens, width)
    return (outgoing * live_rows[:, None, None, None], jnp.take(sources, me_index, axis=0))


def body(activations, out_grads, sign_bits, block_ids):
    shards = lax.axis_size("shard")
    me_index = lax.axis_index("shard")
    tokens = out_grads.shape[0]
    width = BLK
    own_blocks = block_ids.shape[1]
    blocks_per = out_grads.shape[1] // width
    model_width = activations.shape[1] * shards
    inv_block = 1.0 / math.sqrt(width)
    inv_shard = 1.0 / math.sqrt(shards)
    partial_gram = jnp.dot(activations, activations.T, preferred_element_type=jnp.float32)
    token_gram = lax.psum(partial_gram, "shard").astype(jnp.bfloat16)
    sign_values = (1 - 2 * sign_bits).astype(jnp.bfloat16)
    flipped = (out_grads * sign_values[None, :]).reshape(tokens, blocks_per, width)
    block_table = parity_table(width).astype(jnp.bfloat16)
    local_mix = jnp.einsum("tbj,jk->btk", flipped, block_table, preferred_element_type=jnp.float32)
    local_mix = (local_mix * inv_block).astype(jnp.bfloat16)
    running = local_mix.astype(jnp.float32)
    for level in range(shards.bit_length() - 1):
        partner = partner_2(running, "shard", level)
        upper = jnp.right_shift(me_index, level) & 1 == 1
        running = jnp.where(upper, partner - running, running + partner)
    mixed = (running * inv_shard).astype(jnp.bfloat16)
    outgoing, own_sources = route_sampled(
        mixed, block_ids, me_index, shards, blocks_per, tokens, width
    )
    incoming = lax.all_to_all(outgoing, "shard", split_axis=0, concat_axis=0, tiled=True)
    sketched = jnp.take(incoming, own_sources, axis=0).reshape(own_blocks, tokens, width)
    weighted = jnp.einsum(
        "tu,jub->jtb", token_gram, sketched, preferred_element_type=jnp.float32
    ).astype(jnp.bfloat16)
    block_gram = jnp.einsum("jtb,ktc->jbkc", sketched, weighted, preferred_element_type=jnp.float32)
    own_cols = own_blocks * width
    block_gram = block_gram.reshape(own_cols, own_cols)
    summed = lax.psum(block_gram, "dp")
    return summed / (lax.axis_size("dp") * tokens * model_width)


ALONG = pl.DeviceIdType.MESH
COUNT = 8
PIECES = 2 * COUNT
CUTS = 4
GB = 10
TRIANGLE = tuple((i, j) for i in range(4) for j in range(i + 1))
UNITS = COUNT * (COUNT + 1) // 2
ORDER = tuple((1, COUNT - 1) if k == PIECES - 1 else (0, (k + 1) // 2) if k % 2 or k == 0 else (1, k // 2 - 1) for k in range(PIECES))
WHOLE = tuple((j, 0, BLK) for j in range(COUNT))
SPLIT = WHOLE[:-1] + ((COUNT - 1, 0, BLK // 2), (COUNT - 1, BLK // 2, BLK))
CHUNKS = (WHOLE, SPLIT)
STEPS = tuple((t, c, k) for k, (t, j) in enumerate(ORDER) for c, chunk in enumerate(CHUNKS[t]) if chunk[0] == j)


def units_of(chunk):
    j, lo, hi = chunk
    first = j * (j + 1) // 2
    if j < COUNT - 1:
        return first, j + 1
    half = COUNT // 2
    return first + half * (lo // (BLK // 2)), half * ((hi - lo) // (BLK // 2))


def mix_kernel(
    shards, parts, own, per, act_hbm, grads_hbm, bits_hbm, ids_hbm, gathered,
    act, grads, bits, flips, ids, rx, tx, grx, gtx, part, full, sketch, keep, give, prx, rtx, rrx,
    l_sem, z_send, z_recv, p_send, p_recv, r_send, r_recv, f_send, f_recv, a_send, a_recv, w_send, w_recv,
):
    z = lax.axis_index("shard")
    d = lax.axis_index("dp")
    core = lax.rem(d, 2)
    chip = d // 2
    last = shards - 1
    edge = (z == 0) | (z == last)
    middle = jnp.logical_not(edge)
    tokens = act.shape[0]
    width = BLK
    inv_block = 1.0 / math.sqrt(width)
    inv_shard = 1.0 / math.sqrt(shards)
    quarter = width // CUTS
    most = len(CHUNKS[1])

    barrier = pltpu.get_barrier_semaphore()

    def peer(m):
        flipped = 1 - lax.rem(chip, 2) if m & 1 else lax.rem(chip, 2)
        high = 1 - chip // 2 if m & 2 else chip // 2
        return (high * 2 + flipped) * 2 + core

    partner = chip * 2 + 1 - core
    for m in (1, 2, 3):
        pl.semaphore_signal(barrier, inc=1, device_id={"dp": peer(m)}, device_id_type=ALONG)
    pl.semaphore_signal(barrier, inc=1, device_id={"dp": partner}, device_id_type=ALONG)

    @pl.when(z > 0)
    def _():
        pl.semaphore_signal(barrier, inc=1, device_id={"shard": z - 1}, device_id_type=ALONG)

    @pl.when(z < last)
    def _():
        pl.semaphore_signal(barrier, inc=1, device_id={"shard": z + 1}, device_id_type=ALONG)

    loads = (
        pltpu.make_async_copy(act_hbm, act, l_sem.at[0]),
        pltpu.make_async_copy(ids_hbm, ids, l_sem.at[1]),
        pltpu.make_async_copy(bits_hbm, bits, l_sem.at[2]),
    ) + tuple(
        pltpu.make_async_copy(grads_hbm.at[:, pl.ds(width * b, width)], grads.at[b], l_sem.at[3]) for b in range(per)
    )
    for load in loads:
        load.start()

    row = lax.broadcasted_iota(jnp.int32, (width, width), 0)
    col = lax.broadcasted_iota(jnp.int32, (width, width), 1)
    both = row & col
    count = both & 1
    for level in range(1, width.bit_length() - 1):
        count = count + ((both >> level) & 1)
    table = (1 - 2 * (count & 1)).astype(jnp.float32)

    def contribution(owner, j):
        block = ids[owner, j]
        r = lax.div(block, per)
        local = block - r * per
        common = r & z
        odd = common & 1
        for level in range(1, shards.bit_length() - 1):
            odd = odd + ((common >> level) & 1)
        sign = 1 - 2 * (odd & 1)
        signs = flips[local] * sign.astype(jnp.float32)
        lm = lax.dot_general(
            (table * signs).astype(jnp.bfloat16), grads[local], (((1,), (1,)), ((), ())),
            preferred_element_type=jnp.float32)
        return ((lm * inv_block).astype(jnp.bfloat16).astype(jnp.float32) * inv_shard).astype(jnp.bfloat16)

    def owner_of(way, t):
        return jnp.where(way == 0, 1 - t, 2 + t)

    def piece(k):
        if isinstance(k, int):
            return ORDER[k]
        odd = lax.rem(k, 2) == 1
        final = k == PIECES - 1
        t = jnp.where(final | jnp.logical_not(odd | (k == 0)), 1, 0)
        j = jnp.where(final, COUNT - 1, jnp.where(t == 1, k // 2 - 1, (k + 1) // 2))
        return t, j

    def target(way):
        return jnp.where(way == 0, z - 1, z + 1)

    def s_move(way, k, h, who):
        rows = pl.ds(quarter * h, quarter)
        n = GB + CUTS * k + h
        return pltpu.make_async_remote_copy(
            tx.at[way, k, rows], rx.at[way, k, rows], z_send.at[way, 1], z_recv.at[way, n],
            device_id={"shard": who}, device_id_type=ALONG)

    def s_copy(way, k, h):
        return s_move(way, k, h, target(way))

    def g_move(way, n, who):
        return pltpu.make_async_remote_copy(
            gtx.at[way, n], grx.at[way, n], z_send.at[way, 0], z_recv.at[way, n],
            device_id={"shard": who}, device_id_type=ALONG)

    def g_copy(way, n):
        return g_move(way, n, target(way))

    def z_sent(way):
        pltpu.make_async_remote_copy(
            gtx.at[way], grx.at[way], z_send.at[way, 0], z_recv.at[way, 0],
            device_id={"shard": target(way)}, device_id_type=ALONG).wait_send()
        pltpu.make_async_remote_copy(
            tx.at[way], rx.at[way], z_send.at[way, 1], z_recv.at[way, 0],
            device_id={"shard": target(way)}, device_id_type=ALONG).wait_send()

    def gpart(n):
        i, j = TRIANGLE[n]
        return part[128 * i : 128 * (i + 1), 128 * j : 128 * (j + 1)]

    def fill(way, k):
        t, j = piece(k)
        tx[way, k] = contribution(owner_of(way, t), j)

    def units(t, c):
        return pl.ds(*units_of(CHUNKS[t][c]))

    def a_copy(t, c, slot, who):
        arrival = a_recv.at[most] if slot == 3 else a_recv.at[c]
        return pltpu.make_async_remote_copy(
            gathered.at[d, units(t, c)], gathered.at[d, units(t, c)], a_send.at[slot], arrival,
            device_id={"dp": who}, device_id_type=ALONG)

    def w_copy(t, c, m):
        return pltpu.make_async_remote_copy(
            gathered.at[peer(m), units(t, c)], gathered.at[peer(m), units(t, c)],
            w_send.at[0], w_recv.at[0],
            device_id={"dp": partner}, device_id_type=ALONG)

    def spread(t, c):
        for m in (1, 2, 3):
            a_copy(t, c, m - 1, peer(m)).start()
        a_copy(t, c, 3, partner).start()

    def relay(t, c):
        us = units(t, c)
        pltpu.make_async_remote_copy(
            gathered.at[0:3, us], gathered.at[0:3, us], a_send.at[0], a_recv.at[c],
            device_id={"dp": partner}, device_id_type=ALONG).wait_recv()
        for m in (1, 2, 3):
            w_copy(t, c, m).start()

    def settle():
        one = pltpu.make_async_remote_copy(
            gathered.at[0], gathered.at[0], a_send.at[3], a_recv.at[most],
            device_id={"dp": partner}, device_id_type=ALONG)
        three = pltpu.make_async_remote_copy(
            gathered.at[0:3], gathered.at[0:3], w_send.at[0], w_recv.at[0],
            device_id={"dp": partner}, device_id_type=ALONG)
        one.wait_recv()
        three.wait_recv()
        for slot in range(3):
            pltpu.make_async_remote_copy(
                gathered.at[0], gathered.at[0], a_send.at[slot], a_recv.at[0],
                device_id={"dp": partner}, device_id_type=ALONG).wait_send()
        one.wait_send()
        three.wait_send()

    def f_copy(c, who):
        us = units(0, c)
        return pltpu.make_async_remote_copy(
            rrx.at[3, us], gathered.at[d, us], f_send.at[0], f_recv.at[c],
            device_id={"shard": who}, device_id_type=ALONG)

    loads[0].wait()
    part[...] = lax.dot_general(act[...], act[...], (((1,), (1,)), ((), ())), preferred_element_type=jnp.float32)
    loads[1].wait()
    loads[2].wait()
    pltpu.make_async_copy(grads, grads, l_sem.at[3]).wait()
    for b in range(per):
        flips[b] = (1 - 2 * bits[width * b : width * (b + 1)].reshape(1, width)).astype(jnp.float32)

    @pl.when(edge)
    def _():
        pl.semaphore_wait(barrier, 5)

    @pl.when(middle)
    def _():
        pl.semaphore_wait(barrier, 6)

    @pl.when(edge)
    def _():
        out_way = jnp.where(z == 0, 1, 0)
        in_way = 1 - out_way
        side = target(out_way)
        for n in range(GB):
            gtx[out_way, n] = gpart(n).astype(jnp.bfloat16)
            g_copy(out_way, n).start()

        def push(k, carry):
            fill(out_way, k)
            for h in range(CUTS):
                s_copy(out_way, k, h).start()
            return carry

        lax.fori_loop(0, PIECES, push, 0)

        def ready(p, carry):
            t, j = p // COUNT, lax.rem(p, COUNT)
            sketch[t, pl.ds(pl.multiple_of(width * j, width), width)] = contribution(owner_of(in_way, t), j)
            return carry

        lax.fori_loop(0, PIECES, ready, 0)

        for n in range(GB):
            g_move(in_way, n, side).wait_recv()
            r, c = TRIANGLE[n]
            block = (grx[in_way, n].astype(jnp.float32) + gpart(n)).astype(jnp.bfloat16)
            full[128 * r : 128 * (r + 1), 128 * c : 128 * (c + 1)] = block
            if r != c:
                full[128 * c : 128 * (c + 1), 128 * r : 128 * (r + 1)] = block.T

        def where(q):
            t, c, k = STEPS[q]
            first, number = units_of(CHUNKS[t][c])
            return t, c, k, pl.ds(UNITS * t + first, number)

        def p_copy(q):
            t, c, k, us = where(q)
            return pltpu.make_async_remote_copy(
                give.at[us], prx.at[us], p_send.at[0], p_recv.at[q],
                device_id={"dp": partner}, device_id_type=ALONG)

        def r_copy(q, m):
            t, c, k, us = where(q)
            return pltpu.make_async_remote_copy(
                rtx.at[peer(m) // 2, us], rrx.at[m - 1, us], r_send.at[m - 1], r_recv.at[q],
                device_id={"dp": peer(m)}, device_id_type=ALONG)

        def step_a(q):
            t, c, k, us = where(q)
            j, lo, hi = CHUNKS[t][c]
            for h in range(lo // quarter, hi // quarter):
                s_move(in_way, k, h, side).wait_recv()
                rows = slice(width * j + quarter * h, width * j + quarter * (h + 1))
                arrived = rx[in_way, k, quarter * h : quarter * (h + 1)].astype(jnp.float32)
                sketch[t, rows] = (arrived + sketch[t, rows].astype(jnp.float32)).astype(jnp.bfloat16)
            mine = sketch[t, width * j + lo : width * j + hi]
            weighted = jnp.dot(mine, full[...], preferred_element_type=jnp.float32).astype(jnp.bfloat16)
            half = width // 2
            first, number = units_of(CHUNKS[t][c])

            def put(u, top, bottom):
                keep[UNITS * t + u] = jnp.where(core == 0, top, bottom)
                give[UNITS * t + u] = jnp.where(core == 0, bottom, top).astype(jnp.bfloat16)

            for i in range(0, j + 1, 2):
                end = min(i + 2, j + 1)
                block = lax.dot_general(
                    weighted, sketch[t, width * i : width * end], (((1,), (1,)), ((), ())),
                    preferred_element_type=jnp.float32)
                if j < COUNT - 1:
                    for n in range(i, end):
                        cols = slice(width * (n - i), width * (n - i + 1))
                        put(first + n, block[:half, cols], block[half:, cols])
                else:
                    for g in range((hi - lo) // half):
                        rows = slice(half * g, half * (g + 1))
                        put(first + COUNT // 2 * g + i // 2, block[rows, :width], block[rows, width:])
            p_copy(q).start()

        def step_b(q):
            t, c, k, us = where(q)
            p_copy(q).wait_recv()
            total = (keep[us] + prx[us].astype(jnp.float32)).astype(jnp.bfloat16)
            for n in range(4):
                rtx[n, us] = total[:, 16 * n : 16 * (n + 1)]
            for m in (1, 2, 3):
                r_copy(q, m).start()

        def step_c(q):
            t, c, k, us = where(q)
            pltpu.make_async_remote_copy(
                rrx.at[0:3, us], rrx.at[0:3, us], r_send.at[0], r_recv.at[q],
                device_id={"dp": partner}, device_id_type=ALONG).wait_recv()
            total = rtx[chip, us].astype(jnp.float32)
            for m in range(3):
                total = total + rrx[m, us].astype(jnp.float32)
            total = (total * (1.0 / (parts * tokens * act.shape[1] * shards))).astype(jnp.bfloat16)
            if t == 0:
                rrx[3, units(t, c)] = total
                f_copy(c, side).start()
            else:
                gathered[d, units(t, c)] = total
                spread(t, c)

        def step_d(q):
            t, c, k, us = where(q)
            if t == 1:
                relay(t, c)

        def drain():
            pltpu.make_async_remote_copy(
                give, prx, p_send.at[0], p_recv.at[0],
                device_id={"dp": partner}, device_id_type=ALONG).wait_send()
            for m in range(3):
                pltpu.make_async_remote_copy(
                    rtx.at[m], rrx.at[m], r_send.at[m], r_recv.at[0],
                    device_id={"dp": partner}, device_id_type=ALONG).wait_send()
            us = pl.ds(0, UNITS)
            pltpu.make_async_remote_copy(
                rrx.at[3, us], gathered.at[d, us], f_send.at[0], f_recv.at[0],
                device_id={"shard": side}, device_id_type=ALONG).wait_send()
            z_sent(out_way)

        steps = len(STEPS)
        for q in range(steps - 3):
            step_a(q)
            step_b(q)
            if q >= 2:
                step_c(q - 2)
            if q >= 4:
                step_d(q - 4)
        e = steps - 3
        step_a(e)
        step_c(e - 2)
        step_a(e + 1)
        step_b(e)
        step_a(e + 2)
        step_b(e + 1)
        step_c(e - 1)
        step_b(e + 2)
        step_d(e - 4)
        step_d(e - 3)
        step_d(e - 2)
        step_c(e)
        step_c(e + 1)
        step_c(e + 2)
        step_d(e - 1)
        step_d(e)
        step_d(e + 1)
        drain()
        step_d(e + 2)
        settle()

    @pl.when(middle)
    def _():
        near = jnp.where(z == 1, 1, 0)
        far = 1 - near
        outward = jnp.where(z == 1, 0, last)

        def pass_g(way, n):
            g_copy(way, n).wait_recv()
            gtx[way, n] = (grx[way, n].astype(jnp.float32) + gpart(n)).astype(jnp.bfloat16)
            g_copy(way, n).start()

        def pass_s(way, k, h):
            s_copy(way, k, h).wait_recv()
            rows = slice(quarter * h, quarter * (h + 1))
            tx[way, k, rows] = (rx[way, k, rows].astype(jnp.float32) + tx[way, k, rows].astype(jnp.float32)).astype(jnp.bfloat16)
            s_copy(way, k, h).start()

        lag = CUTS + 1
        for n in range(GB):
            pass_g(near, n)
            if n >= lag:
                pass_g(far, n - lag)
        fill(near, 0)
        for h in range(CUTS):
            pass_s(near, 0, h)
            pass_g(far, GB - lag + h)
        fill(near, 1)
        fill(far, 0)
        pass_s(near, 1, 0)
        pass_g(far, GB - 1)
        for h in range(1, CUTS):
            pass_s(near, 1, h)
            pass_s(far, 0, h - 1)

        def both_ways(k, carry):
            fill(near, k)
            fill(far, k - 1)
            pass_s(near, k, 0)
            pass_s(far, k - 2, CUTS - 1)
            for h in range(1, CUTS):
                pass_s(near, k, h)
                pass_s(far, k - 1, h - 1)
            return carry

        lax.fori_loop(2, PIECES, both_ways, 0)
        fill(far, PIECES - 1)
        pass_s(far, PIECES - 2, CUTS - 1)
        for h in range(CUTS):
            pass_s(far, PIECES - 1, h)

        chunks = len(CHUNKS[0])
        for c in range(chunks):
            f_copy(c, outward).wait_recv()
            spread(0, c)
            if c >= 2:
                relay(0, c - 2)
        z_sent(near)
        z_sent(far)
        relay(0, chunks - 2)
        relay(0, chunks - 1)
        settle()


def assemble_kernel(got, out, held, sems):
    half = BLK // 2

    def unit(u):
        rows = [got[2 * n + h, u] for h in range(2) for n in range(4)]
        return jnp.concatenate(rows, axis=0).astype(jnp.float32)

    def put(i):
        rows = pl.ds(BLK * i, BLK)
        return pltpu.make_async_copy(held.at[rows], out.at[rows], sems.at[i])

    final = COUNT - 1
    first = final * COUNT // 2
    lower = {}
    for v in range(COUNT // 2):
        top, bottom = unit(first + v), unit(first + COUNT // 2 + v)
        for g in range(2):
            rows = slice(half * g, half * (g + 1))
            lower[2 * v + g] = jnp.concatenate([top[rows], bottom[rows]], axis=0)
    square = lower[final]
    row = lax.broadcasted_iota(jnp.int32, (BLK, BLK), 0)
    col = lax.broadcasted_iota(jnp.int32, (BLK, BLK), 1)
    lower[final] = jnp.where((row < half) & (col >= half), square.T, square)
    for i in range(COUNT):
        for j in range(COUNT):
            if i == final:
                block = lower[j]
            elif j == final:
                block = lower[i].T
            elif j <= i:
                block = unit(i * (i + 1) // 2 + j)
            else:
                block = unit(j * (j + 1) // 2 + i).T
            held[BLK * i : BLK * (i + 1), BLK * j : BLK * (j + 1)] = block
        put(i).start()
    for i in range(COUNT):
        put(i).wait()


def fast_body(shards, parts, activations, out_grads, sign_bits, block_ids):
    tokens, columns = out_grads.shape
    per = columns // BLK
    own = block_ids.shape[1]
    vmem = pl.BlockSpec(memory_space=pltpu.VMEM)
    hbm = pl.BlockSpec(memory_space=pltpu.HBM)
    bf, f32 = jnp.bfloat16, jnp.float32
    dma = pltpu.SemaphoreType.DMA
    steps, most = len(STEPS), len(CHUNKS[1])
    got = pl.pallas_call(
        functools.partial(mix_kernel, shards, parts, own, per),
        out_shape=jax.ShapeDtypeStruct((parts, UNITS, 16, BLK), bf),
        in_specs=[hbm, hbm, hbm, hbm],
        out_specs=vmem,
        scratch_shapes=[
            pltpu.VMEM(activations.shape, bf),
            pltpu.VMEM((per, tokens, BLK), bf),
            pltpu.VMEM(sign_bits.shape, jnp.int32),
            pltpu.VMEM((per, 1, BLK), f32),
            pltpu.SMEM(block_ids.shape, jnp.int32),
            pltpu.VMEM((2, PIECES, BLK, tokens), bf),
            pltpu.VMEM((2, PIECES, BLK, tokens), bf),
            pltpu.VMEM((2, GB, 128, 128), bf),
            pltpu.VMEM((2, GB, 128, 128), bf),
            pltpu.VMEM((tokens, tokens), f32),
            pltpu.VMEM((tokens, tokens), bf),
            pltpu.VMEM((2, own * BLK, tokens), bf),
            pltpu.VMEM((2 * UNITS, 64, BLK), f32),
            pltpu.VMEM((2 * UNITS, 64, BLK), bf),
            pltpu.VMEM((2 * UNITS, 64, BLK), bf),
            pltpu.VMEM((4, 2 * UNITS, 16, BLK), bf),
            pltpu.VMEM((4, 2 * UNITS, 16, BLK), bf),
            dma((4,)),
            dma((2, 2)), dma((2, GB + CUTS * PIECES)),
            dma((1,)), dma((steps,)),
            dma((3,)), dma((steps,)),
            dma((1,)), dma((COUNT,)),
            dma((4,)), dma((most + 1,)),
            dma((1,)), dma((1,)),
        ],
        compiler_params=pltpu.CompilerParams(collective_id=0, has_side_effects=True, vmem_limit_bytes=50 * 2**20),
        name="mix",
    )(activations, out_grads, sign_bits, block_ids)
    return pl.pallas_call(
        assemble_kernel,
        out_shape=jax.ShapeDtypeStruct((own * BLK, own * BLK), f32),
        in_specs=[vmem],
        out_specs=hbm,
        scratch_shapes=[pltpu.VMEM((own * BLK, own * BLK), f32), dma((own,))],
        compiler_params=pltpu.CompilerParams(vmem_limit_bytes=16 * 2**20),
        name="assemble",
    )(got)


def solution(mesh):
    in_specs = (P("dp", "shard"), P("dp", "shard"), P("shard"), P())
    out_specs = P("shard", None)
    shards, parts = mesh.shape["shard"], mesh.shape["dp"]
    chosen = functools.partial(fast_body, shards, parts) if (shards, parts) == (4, 8) else body
    return jax.shard_map(chosen, mesh=mesh, in_specs=in_specs, out_specs=out_specs, check_vma=False)
```

```python
import functools
import math

import jax
import jax.numpy as jnp
from jax import lax
from jax.experimental import pallas as pl
from jax.experimental.pallas import tpu as pltpu
from jax.sharding import PartitionSpec as P

BLK = 128
CAP = 2


def partner_2(x, axis, distance):
    return lax.ppermute(x, axis, [(i, i ^ 1 << distance) for i in range(lax.axis_size(axis))])


def parity_table(count):
    index = jnp.arange(count, dtype=jnp.int32)
    total = jnp.zeros((count, count), jnp.int32)
    for level in range(count.bit_length() - 1):
        total = total + (
            jnp.right_shift(index[:, None], level) & jnp.right_shift(index[None, :], level) & 1
        )
    return (1 - 2 * (total % 2)).astype(jnp.float32)


def route_sampled(mixed, block_ids, me_index, shards, blocks_per, tokens, width):
    groups = block_ids.shape[1] // CAP
    sources = block_ids[:, ::CAP] // blocks_per
    local_ids = (block_ids % blocks_per).reshape(shards, groups, CAP)
    matched = sources == me_index
    chosen = jnp.sum(jnp.where(matched[:, :, None], local_ids, 0), axis=1)
    live_rows = jnp.any(matched, axis=1).astype(jnp.bfloat16)
    outgoing = jnp.take(mixed, chosen.reshape(-1), axis=0).reshape(shards, CAP, tokens, width)
    return (outgoing * live_rows[:, None, None, None], jnp.take(sources, me_index, axis=0))


def body(activations, out_grads, sign_bits, block_ids):
    shards = lax.axis_size("shard")
    me_index = lax.axis_index("shard")
    tokens = out_grads.shape[0]
    width = BLK
    own_blocks = block_ids.shape[1]
    blocks_per = out_grads.shape[1] // width
    model_width = activations.shape[1] * shards
    inv_block = 1.0 / math.sqrt(width)
    inv_shard = 1.0 / math.sqrt(shards)
    partial_gram = jnp.dot(activations, activations.T, preferred_element_type=jnp.float32)
    token_gram = lax.psum(partial_gram, "shard").astype(jnp.bfloat16)
    sign_values = (1 - 2 * sign_bits).astype(jnp.bfloat16)
    flipped = (out_grads * sign_values[None, :]).reshape(tokens, blocks_per, width)
    block_table = parity_table(width).astype(jnp.bfloat16)
    local_mix = jnp.einsum("tbj,jk->btk", flipped, block_table, preferred_element_type=jnp.float32)
    local_mix = (local_mix * inv_block).astype(jnp.bfloat16)
    running = local_mix.astype(jnp.float32)
    for level in range(shards.bit_length() - 1):
        partner = partner_2(running, "shard", level)
        upper = jnp.right_shift(me_index, level) & 1 == 1
        running = jnp.where(upper, partner - running, running + partner)
    mixed = (running * inv_shard).astype(jnp.bfloat16)
    outgoing, own_sources = route_sampled(
        mixed, block_ids, me_index, shards, blocks_per, tokens, width
    )
    incoming = lax.all_to_all(outgoing, "shard", split_axis=0, concat_axis=0, tiled=True)
    sketched = jnp.take(incoming, own_sources, axis=0).reshape(own_blocks, tokens, width)
    weighted = jnp.einsum(
        "tu,jub->jtb", token_gram, sketched, preferred_element_type=jnp.float32
    ).astype(jnp.bfloat16)
    block_gram = jnp.einsum("jtb,ktc->jbkc", sketched, weighted, preferred_element_type=jnp.float32)
    own_cols = own_blocks * width
    block_gram = block_gram.reshape(own_cols, own_cols)
    summed = lax.psum(block_gram, "dp")
    return summed / (lax.axis_size("dp") * tokens * model_width)


ALONG = pl.DeviceIdType.MESH
COUNT = 8
PIECES = 2 * COUNT
CUTS = 4
GB = 9
BELOW = tuple((i, j) for i in range(4) for j in range(i))
ROWS = tuple(128 if n < GB - 1 else 16 for n in range(GB))
UNITS = COUNT * (COUNT + 1) // 2
ORDER = tuple((1, COUNT - 1) if k == PIECES - 1 else (0, (k + 1) // 2) if k % 2 or k == 0 else (1, k // 2 - 1) for k in range(PIECES))
WHOLE = tuple((j, 0, BLK) for j in range(COUNT))
SPLIT = WHOLE[:-1] + ((COUNT - 1, 0, BLK // 2), (COUNT - 1, BLK // 2, BLK))
CHUNKS = (WHOLE, SPLIT)
STEPS = tuple((t, c, k) for k, (t, j) in enumerate(ORDER) for c, chunk in enumerate(CHUNKS[t]) if chunk[0] == j)


def units_of(chunk):
    j, lo, hi = chunk
    first = j * (j + 1) // 2
    if j < COUNT - 1:
        return first, j + 1
    half = COUNT // 2
    return first + half * (lo // (BLK // 2)), half * ((hi - lo) // (BLK // 2))


def mix_kernel(
    shards, parts, own, per, act_hbm, grads_hbm, bits_hbm, ids_hbm, gathered,
    act, grads, bits, flips, ids, rx, tx, grx, gtx, part, pairs, diagonals, full, sketch, keep, give, prx, rtx, rrx,
    l_sem, z_send, z_recv, p_send, p_recv, r_send, r_recv, f_send, f_recv, a_send, a_recv, w_send, w_recv,
):
    z = lax.axis_index("shard")
    d = lax.axis_index("dp")
    core = lax.rem(d, 2)
    chip = d // 2
    last = shards - 1
    edge = (z == 0) | (z == last)
    middle = jnp.logical_not(edge)
    tokens = act.shape[0]
    width = BLK
    inv_block = 1.0 / math.sqrt(width)
    inv_shard = 1.0 / math.sqrt(shards)
    quarter = width // CUTS
    most = len(CHUNKS[1])

    barrier = pltpu.get_barrier_semaphore()

    def peer(m):
        flipped = 1 - lax.rem(chip, 2) if m & 1 else lax.rem(chip, 2)
        high = 1 - chip // 2 if m & 2 else chip // 2
        return (high * 2 + flipped) * 2 + core

    partner = chip * 2 + 1 - core
    for m in (1, 2, 3):
        pl.semaphore_signal(barrier, inc=1, device_id={"dp": peer(m)}, device_id_type=ALONG)
    pl.semaphore_signal(barrier, inc=1, device_id={"dp": partner}, device_id_type=ALONG)

    @pl.when(z > 0)
    def _():
        pl.semaphore_signal(barrier, inc=1, device_id={"shard": z - 1}, device_id_type=ALONG)

    @pl.when(z < last)
    def _():
        pl.semaphore_signal(barrier, inc=1, device_id={"shard": z + 1}, device_id_type=ALONG)

    loads = (
        pltpu.make_async_copy(act_hbm, act, l_sem.at[0]),
        pltpu.make_async_copy(ids_hbm, ids, l_sem.at[1]),
        pltpu.make_async_copy(bits_hbm, bits, l_sem.at[2]),
    ) + tuple(
        pltpu.make_async_copy(grads_hbm.at[:, pl.ds(width * b, width)], grads.at[b], l_sem.at[3]) for b in range(per)
    )
    for load in loads:
        load.start()

    row = lax.broadcasted_iota(jnp.int32, (width, width), 0)
    col = lax.broadcasted_iota(jnp.int32, (width, width), 1)
    both = row & col
    count = both & 1
    for level in range(1, width.bit_length() - 1):
        count = count + ((both >> level) & 1)
    table = (1 - 2 * (count & 1)).astype(jnp.float32)

    def contribution(owner, j):
        block = ids[owner, j]
        r = lax.div(block, per)
        local = block - r * per
        common = r & z
        odd = common & 1
        for level in range(1, shards.bit_length() - 1):
            odd = odd + ((common >> level) & 1)
        sign = 1 - 2 * (odd & 1)
        signs = flips[local] * sign.astype(jnp.float32)
        lm = lax.dot_general(
            (table * signs).astype(jnp.bfloat16), grads[local], (((1,), (1,)), ((), ())),
            preferred_element_type=jnp.float32)
        return ((lm * inv_block).astype(jnp.bfloat16).astype(jnp.float32) * inv_shard).astype(jnp.bfloat16)

    def owner_of(way, t):
        return jnp.where(way == 0, 1 - t, 2 + t)

    def piece(k):
        if isinstance(k, int):
            return ORDER[k]
        odd = lax.rem(k, 2) == 1
        final = k == PIECES - 1
        t = jnp.where(final | jnp.logical_not(odd | (k == 0)), 1, 0)
        j = jnp.where(final, COUNT - 1, jnp.where(t == 1, k // 2 - 1, (k + 1) // 2))
        return t, j

    def target(way):
        return jnp.where(way == 0, z - 1, z + 1)

    def s_move(way, k, h, who):
        rows = pl.ds(quarter * h, quarter)
        n = GB + CUTS * k + h
        return pltpu.make_async_remote_copy(
            tx.at[way, k, rows], rx.at[way, k, rows], z_send.at[way, 1], z_recv.at[way, n],
            device_id={"shard": who}, device_id_type=ALONG)

    def s_copy(way, k, h):
        return s_move(way, k, h, target(way))

    def g_move(way, n, who):
        rows = pl.ds(0, ROWS[n])
        return pltpu.make_async_remote_copy(
            gtx.at[way, n, rows], grx.at[way, n, rows], z_send.at[way, 2 * (n // (GB - 1))], z_recv.at[way, n],
            device_id={"shard": who}, device_id_type=ALONG)

    def g_copy(way, n):
        return g_move(way, n, target(way))

    def z_sent(way):
        pltpu.make_async_remote_copy(
            gtx.at[way, 0 : GB - 1], grx.at[way, 0 : GB - 1], z_send.at[way, 0], z_recv.at[way, 0],
            device_id={"shard": target(way)}, device_id_type=ALONG).wait_send()
        g_copy(way, GB - 1).wait_send()
        pltpu.make_async_remote_copy(
            tx.at[way], rx.at[way], z_send.at[way, 1], z_recv.at[way, 0],
            device_id={"shard": target(way)}, device_id_type=ALONG).wait_send()

    def square(i, j):
        return part[128 * i : 128 * (i + 1), 128 * j : 128 * (j + 1)]

    def gpart(n):
        if n < len(BELOW):
            return square(*BELOW[n])
        if n < GB - 1:
            return pairs[n - len(BELOW)]
        return diagonals[...]

    def gsum(way, n):
        return (grx[way, n, : ROWS[n]].astype(jnp.float32) + gpart(n)).astype(jnp.bfloat16)

    def fill(way, k):
        t, j = piece(k)
        tx[way, k] = contribution(owner_of(way, t), j)

    def units(t, c):
        return pl.ds(*units_of(CHUNKS[t][c]))

    def a_copy(t, c, slot, who):
        arrival = a_recv.at[most] if slot == 3 else a_recv.at[c]
        return pltpu.make_async_remote_copy(
            gathered.at[d, units(t, c)], gathered.at[d, units(t, c)], a_send.at[slot], arrival,
            device_id={"dp": who}, device_id_type=ALONG)

    def w_copy(t, c, m):
        return pltpu.make_async_remote_copy(
            gathered.at[peer(m), units(t, c)], gathered.at[peer(m), units(t, c)],
            w_send.at[0], w_recv.at[0],
            device_id={"dp": partner}, device_id_type=ALONG)

    def spread(t, c):
        for m in (1, 2, 3):
            a_copy(t, c, m - 1, peer(m)).start()
        a_copy(t, c, 3, partner).start()

    def relay(t, c):
        us = units(t, c)
        pltpu.make_async_remote_copy(
            gathered.at[0:3, us], gathered.at[0:3, us], a_send.at[0], a_recv.at[c],
            device_id={"dp": partner}, device_id_type=ALONG).wait_recv()
        for m in (1, 2, 3):
            w_copy(t, c, m).start()

    def settle():
        one = pltpu.make_async_remote_copy(
            gathered.at[0], gathered.at[0], a_send.at[3], a_recv.at[most],
            device_id={"dp": partner}, device_id_type=ALONG)
        three = pltpu.make_async_remote_copy(
            gathered.at[0:3], gathered.at[0:3], w_send.at[0], w_recv.at[0],
            device_id={"dp": partner}, device_id_type=ALONG)
        one.wait_recv()
        three.wait_recv()
        for slot in range(3):
            pltpu.make_async_remote_copy(
                gathered.at[0], gathered.at[0], a_send.at[slot], a_recv.at[0],
                device_id={"dp": partner}, device_id_type=ALONG).wait_send()
        one.wait_send()
        three.wait_send()

    def f_copy(c, who):
        us = units(0, c)
        return pltpu.make_async_remote_copy(
            rrx.at[3, us], gathered.at[d, us], f_send.at[0], f_recv.at[c],
            device_id={"shard": who}, device_id_type=ALONG)

    loads[0].wait()
    part[...] = lax.dot_general(act[...], act[...], (((1,), (1,)), ((), ())), preferred_element_type=jnp.float32)
    diagonals[...] = jnp.zeros_like(diagonals)
    for n in range(2):
        second = square(2 * n + 1, 2 * n + 1)
        pairs[n] = jnp.where(row >= col, square(2 * n, 2 * n), second)
        diagonals[n : n + 1] = jnp.sum(jnp.where(row == col, second, 0.0), axis=0, keepdims=True)
    loads[1].wait()
    loads[2].wait()
    pltpu.make_async_copy(grads, grads, l_sem.at[3]).wait()
    for b in range(per):
        flips[b] = (1 - 2 * bits[width * b : width * (b + 1)].reshape(1, width)).astype(jnp.float32)

    @pl.when(edge)
    def _():
        pl.semaphore_wait(barrier, 5)

    @pl.when(middle)
    def _():
        pl.semaphore_wait(barrier, 6)

    @pl.when(edge)
    def _():
        out_way = jnp.where(z == 0, 1, 0)
        in_way = 1 - out_way
        side = target(out_way)
        for n in range(GB):
            gtx[out_way, n, : ROWS[n]] = gpart(n).astype(jnp.bfloat16)
            g_copy(out_way, n).start()

        def push(k, carry):
            fill(out_way, k)
            for h in range(CUTS):
                s_copy(out_way, k, h).start()
            return carry

        lax.fori_loop(0, PIECES, push, 0)

        def ready(p, carry):
            t, j = p // COUNT, lax.rem(p, COUNT)
            sketch[t, pl.ds(pl.multiple_of(width * j, width), width)] = contribution(owner_of(in_way, t), j)
            return carry

        lax.fori_loop(0, PIECES, ready, 0)

        for n in range(GB):
            g_move(in_way, n, side).wait_recv()
            if n < len(BELOW):
                r, c = BELOW[n]
                block = gsum(in_way, n)
                full[128 * r : 128 * (r + 1), 128 * c : 128 * (c + 1)] = block
                full[128 * c : 128 * (c + 1), 128 * r : 128 * (r + 1)] = block.T
        ends = gsum(in_way, GB - 1).astype(jnp.float32)
        for n in range(2):
            both_of = gsum(in_way, len(BELOW) + n).astype(jnp.float32)
            turned = both_of.T
            first = jnp.where(row >= col, both_of, turned)
            second = jnp.where(row < col, both_of, jnp.where(row > col, turned, ends[n : n + 1]))
            for i, block in ((2 * n, first), (2 * n + 1, second)):
                full[128 * i : 128 * (i + 1), 128 * i : 128 * (i + 1)] = block.astype(jnp.bfloat16)

        def where(q):
            t, c, k = STEPS[q]
            first, number = units_of(CHUNKS[t][c])
            return t, c, k, pl.ds(UNITS * t + first, number)

        def p_copy(q):
            t, c, k, us = where(q)
            return pltpu.make_async_remote_copy(
                give.at[us], prx.at[us], p_send.at[0], p_recv.at[q],
                device_id={"dp": partner}, device_id_type=ALONG)

        def r_copy(q, m):
            t, c, k, us = where(q)
            return pltpu.make_async_remote_copy(
                rtx.at[peer(m) // 2, us], rrx.at[m - 1, us], r_send.at[m - 1], r_recv.at[q],
                device_id={"dp": peer(m)}, device_id_type=ALONG)

        def step_a(q):
            t, c, k, us = where(q)
            j, lo, hi = CHUNKS[t][c]
            for h in range(lo // quarter, hi // quarter):
                s_move(in_way, k, h, side).wait_recv()
                rows = slice(width * j + quarter * h, width * j + quarter * (h + 1))
                arrived = rx[in_way, k, quarter * h : quarter * (h + 1)].astype(jnp.float32)
                sketch[t, rows] = (arrived + sketch[t, rows].astype(jnp.float32)).astype(jnp.bfloat16)
            mine = sketch[t, width * j + lo : width * j + hi]
            weighted = jnp.dot(mine, full[...], preferred_element_type=jnp.float32).astype(jnp.bfloat16)
            half = width // 2
            first, number = units_of(CHUNKS[t][c])

            def put(u, top, bottom):
                keep[UNITS * t + u] = jnp.where(core == 0, top, bottom)
                give[UNITS * t + u] = jnp.where(core == 0, bottom, top).astype(jnp.bfloat16)

            for i in range(0, j + 1, 2):
                end = min(i + 2, j + 1)
                block = lax.dot_general(
                    weighted, sketch[t, width * i : width * end], (((1,), (1,)), ((), ())),
                    preferred_element_type=jnp.float32)
                if j < COUNT - 1:
                    for n in range(i, end):
                        cols = slice(width * (n - i), width * (n - i + 1))
                        put(first + n, block[:half, cols], block[half:, cols])
                else:
                    for g in range((hi - lo) // half):
                        rows = slice(half * g, half * (g + 1))
                        put(first + COUNT // 2 * g + i // 2, block[rows, :width], block[rows, width:])
            p_copy(q).start()

        def step_b(q):
            t, c, k, us = where(q)
            p_copy(q).wait_recv()
            total = (keep[us] + prx[us].astype(jnp.float32)).astype(jnp.bfloat16)
            for n in range(4):
                rtx[n, us] = total[:, 16 * n : 16 * (n + 1)]
            for m in (1, 2, 3):
                r_copy(q, m).start()

        def step_c(q):
            t, c, k, us = where(q)
            pltpu.make_async_remote_copy(
                rrx.at[0:3, us], rrx.at[0:3, us], r_send.at[0], r_recv.at[q],
                device_id={"dp": partner}, device_id_type=ALONG).wait_recv()
            total = rtx[chip, us].astype(jnp.float32)
            for m in range(3):
                total = total + rrx[m, us].astype(jnp.float32)
            total = (total * (1.0 / (parts * tokens * act.shape[1] * shards))).astype(jnp.bfloat16)
            if t == 0:
                rrx[3, units(t, c)] = total
                f_copy(c, side).start()
            else:
                gathered[d, units(t, c)] = total
                spread(t, c)

        def step_d(q):
            t, c, k, us = where(q)
            if t == 1:
                relay(t, c)

        def drain():
            pltpu.make_async_remote_copy(
                give, prx, p_send.at[0], p_recv.at[0],
                device_id={"dp": partner}, device_id_type=ALONG).wait_send()
            for m in range(3):
                pltpu.make_async_remote_copy(
                    rtx.at[m], rrx.at[m], r_send.at[m], r_recv.at[0],
                    device_id={"dp": partner}, device_id_type=ALONG).wait_send()
            us = pl.ds(0, UNITS)
            pltpu.make_async_remote_copy(
                rrx.at[3, us], gathered.at[d, us], f_send.at[0], f_recv.at[0],
                device_id={"shard": side}, device_id_type=ALONG).wait_send()
            z_sent(out_way)

        steps = len(STEPS)
        for q in range(steps - 3):
            step_a(q)
            step_b(q)
            if q >= 2:
                step_c(q - 2)
            if q >= 4:
                step_d(q - 4)
        e = steps - 3
        step_a(e)
        step_c(e - 2)
        step_a(e + 1)
        step_b(e)
        step_a(e + 2)
        step_b(e + 1)
        step_c(e - 1)
        step_b(e + 2)
        step_d(e - 4)
        step_d(e - 3)
        step_d(e - 2)
        step_c(e)
        step_c(e + 1)
        step_c(e + 2)
        step_d(e - 1)
        step_d(e)
        step_d(e + 1)
        drain()
        step_d(e + 2)
        settle()

    @pl.when(middle)
    def _():
        near = jnp.where(z == 1, 1, 0)
        far = 1 - near
        outward = jnp.where(z == 1, 0, last)

        def pass_g(way, n):
            g_copy(way, n).wait_recv()
            gtx[way, n, : ROWS[n]] = gsum(way, n)
            g_copy(way, n).start()

        def pass_s(way, k, h):
            s_copy(way, k, h).wait_recv()
            rows = slice(quarter * h, quarter * (h + 1))
            tx[way, k, rows] = (rx[way, k, rows].astype(jnp.float32) + tx[way, k, rows].astype(jnp.float32)).astype(jnp.bfloat16)
            s_copy(way, k, h).start()

        lag = CUTS + 1
        for n in range(GB):
            pass_g(near, n)
            if n >= lag:
                pass_g(far, n - lag)
        fill(near, 0)
        for h in range(CUTS):
            pass_s(near, 0, h)
            pass_g(far, GB - lag + h)
        fill(near, 1)
        fill(far, 0)
        pass_s(near, 1, 0)
        pass_g(far, GB - 1)
        for h in range(1, CUTS):
            pass_s(near, 1, h)
            pass_s(far, 0, h - 1)

        def both_ways(k, carry):
            fill(near, k)
            fill(far, k - 1)
            pass_s(near, k, 0)
            pass_s(far, k - 2, CUTS - 1)
            for h in range(1, CUTS):
                pass_s(near, k, h)
                pass_s(far, k - 1, h - 1)
            return carry

        lax.fori_loop(2, PIECES, both_ways, 0)
        fill(far, PIECES - 1)
        pass_s(far, PIECES - 2, CUTS - 1)
        for h in range(CUTS):
            pass_s(far, PIECES - 1, h)

        chunks = len(CHUNKS[0])
        for c in range(chunks):
            f_copy(c, outward).wait_recv()
            spread(0, c)
            if c >= 2:
                relay(0, c - 2)
        z_sent(near)
        z_sent(far)
        relay(0, chunks - 2)
        relay(0, chunks - 1)
        settle()


def assemble_kernel(got, out, held, sems):
    half = BLK // 2

    def unit(u):
        rows = [got[2 * n + h, u] for h in range(2) for n in range(4)]
        return jnp.concatenate(rows, axis=0).astype(jnp.float32)

    def put(i):
        rows = pl.ds(BLK * i, BLK)
        return pltpu.make_async_copy(held.at[rows], out.at[rows], sems.at[i])

    final = COUNT - 1
    first = final * COUNT // 2
    lower = {}
    for v in range(COUNT // 2):
        top, bottom = unit(first + v), unit(first + COUNT // 2 + v)
        for g in range(2):
            rows = slice(half * g, half * (g + 1))
            lower[2 * v + g] = jnp.concatenate([top[rows], bottom[rows]], axis=0)
    square = lower[final]
    row = lax.broadcasted_iota(jnp.int32, (BLK, BLK), 0)
    col = lax.broadcasted_iota(jnp.int32, (BLK, BLK), 1)
    lower[final] = jnp.where((row < half) & (col >= half), square.T, square)
    for i in range(COUNT):
        for j in range(COUNT):
            if i == final:
                block = lower[j]
            elif j == final:
                block = lower[i].T
            elif j <= i:
                block = unit(i * (i + 1) // 2 + j)
            else:
                block = unit(j * (j + 1) // 2 + i).T
            held[BLK * i : BLK * (i + 1), BLK * j : BLK * (j + 1)] = block
        put(i).start()
    for i in range(COUNT):
        put(i).wait()


def fast_body(shards, parts, activations, out_grads, sign_bits, block_ids):
    tokens, columns = out_grads.shape
    per = columns // BLK
    own = block_ids.shape[1]
    vmem = pl.BlockSpec(memory_space=pltpu.VMEM)
    hbm = pl.BlockSpec(memory_space=pltpu.HBM)
    bf, f32 = jnp.bfloat16, jnp.float32
    dma = pltpu.SemaphoreType.DMA
    steps, most = len(STEPS), len(CHUNKS[1])
    got = pl.pallas_call(
        functools.partial(mix_kernel, shards, parts, own, per),
        out_shape=jax.ShapeDtypeStruct((parts, UNITS, 16, BLK), bf),
        in_specs=[hbm, hbm, hbm, hbm],
        out_specs=vmem,
        scratch_shapes=[
            pltpu.VMEM(activations.shape, bf),
            pltpu.VMEM((per, tokens, BLK), bf),
            pltpu.VMEM(sign_bits.shape, jnp.int32),
            pltpu.VMEM((per, 1, BLK), f32),
            pltpu.SMEM(block_ids.shape, jnp.int32),
            pltpu.VMEM((2, PIECES, BLK, tokens), bf),
            pltpu.VMEM((2, PIECES, BLK, tokens), bf),
            pltpu.VMEM((2, GB, 128, 128), bf),
            pltpu.VMEM((2, GB, 128, 128), bf),
            pltpu.VMEM((tokens, tokens), f32),
            pltpu.VMEM((2, 128, 128), f32),
            pltpu.VMEM((16, 128), f32),
            pltpu.VMEM((tokens, tokens), bf),
            pltpu.VMEM((2, own * BLK, tokens), bf),
            pltpu.VMEM((2 * UNITS, 64, BLK), f32),
            pltpu.VMEM((2 * UNITS, 64, BLK), bf),
            pltpu.VMEM((2 * UNITS, 64, BLK), bf),
            pltpu.VMEM((4, 2 * UNITS, 16, BLK), bf),
            pltpu.VMEM((4, 2 * UNITS, 16, BLK), bf),
            dma((4,)),
            dma((2, 3)), dma((2, GB + CUTS * PIECES)),
            dma((1,)), dma((steps,)),
            dma((3,)), dma((steps,)),
            dma((1,)), dma((COUNT,)),
            dma((4,)), dma((most + 1,)),
            dma((1,)), dma((1,)),
        ],
        compiler_params=pltpu.CompilerParams(collective_id=0, has_side_effects=True, vmem_limit_bytes=50 * 2**20),
        name="mix",
    )(activations, out_grads, sign_bits, block_ids)
    return pl.pallas_call(
        assemble_kernel,
        out_shape=jax.ShapeDtypeStruct((own * BLK, own * BLK), f32),
        in_specs=[vmem],
        out_specs=hbm,
        scratch_shapes=[pltpu.VMEM((own * BLK, own * BLK), f32), dma((own,))],
        compiler_params=pltpu.CompilerParams(vmem_limit_bytes=16 * 2**20),
        name="assemble",
    )(got)


def solution(mesh):
    in_specs = (P("dp", "shard"), P("dp", "shard"), P("shard"), P())
    out_specs = P("shard", None)
    shards, parts = mesh.shape["shard"], mesh.shape["dp"]
    chosen = functools.partial(fast_body, shards, parts) if (shards, parts) == (4, 8) else body
    return jax.shard_map(chosen, mesh=mesh, in_specs=in_specs, out_specs=out_specs, check_vma=False)
```

```python
import functools
import math

import jax
import jax.numpy as jnp
from jax import lax
from jax.experimental import pallas as pl
from jax.experimental.pallas import tpu as pltpu
from jax.sharding import PartitionSpec as P

BLK = 128
CAP = 2


def partner_2(x, axis, distance):
    return lax.ppermute(x, axis, [(i, i ^ 1 << distance) for i in range(lax.axis_size(axis))])


def parity_table(count):
    index = jnp.arange(count, dtype=jnp.int32)
    total = jnp.zeros((count, count), jnp.int32)
    for level in range(count.bit_length() - 1):
        total = total + (
            jnp.right_shift(index[:, None], level) & jnp.right_shift(index[None, :], level) & 1
        )
    return (1 - 2 * (total % 2)).astype(jnp.float32)


def route_sampled(mixed, block_ids, me_index, shards, blocks_per, tokens, width):
    groups = block_ids.shape[1] // CAP
    sources = block_ids[:, ::CAP] // blocks_per
    local_ids = (block_ids % blocks_per).reshape(shards, groups, CAP)
    matched = sources == me_index
    chosen = jnp.sum(jnp.where(matched[:, :, None], local_ids, 0), axis=1)
    live_rows = jnp.any(matched, axis=1).astype(jnp.bfloat16)
    outgoing = jnp.take(mixed, chosen.reshape(-1), axis=0).reshape(shards, CAP, tokens, width)
    return (outgoing * live_rows[:, None, None, None], jnp.take(sources, me_index, axis=0))


def body(activations, out_grads, sign_bits, block_ids):
    shards = lax.axis_size("shard")
    me_index = lax.axis_index("shard")
    tokens = out_grads.shape[0]
    width = BLK
    own_blocks = block_ids.shape[1]
    blocks_per = out_grads.shape[1] // width
    model_width = activations.shape[1] * shards
    inv_block = 1.0 / math.sqrt(width)
    inv_shard = 1.0 / math.sqrt(shards)
    partial_gram = jnp.dot(activations, activations.T, preferred_element_type=jnp.float32)
    token_gram = lax.psum(partial_gram, "shard").astype(jnp.bfloat16)
    sign_values = (1 - 2 * sign_bits).astype(jnp.bfloat16)
    flipped = (out_grads * sign_values[None, :]).reshape(tokens, blocks_per, width)
    block_table = parity_table(width).astype(jnp.bfloat16)
    local_mix = jnp.einsum("tbj,jk->btk", flipped, block_table, preferred_element_type=jnp.float32)
    local_mix = (local_mix * inv_block).astype(jnp.bfloat16)
    running = local_mix.astype(jnp.float32)
    for level in range(shards.bit_length() - 1):
        partner = partner_2(running, "shard", level)
        upper = jnp.right_shift(me_index, level) & 1 == 1
        running = jnp.where(upper, partner - running, running + partner)
    mixed = (running * inv_shard).astype(jnp.bfloat16)
    outgoing, own_sources = route_sampled(
        mixed, block_ids, me_index, shards, blocks_per, tokens, width
    )
    incoming = lax.all_to_all(outgoing, "shard", split_axis=0, concat_axis=0, tiled=True)
    sketched = jnp.take(incoming, own_sources, axis=0).reshape(own_blocks, tokens, width)
    weighted = jnp.einsum(
        "tu,jub->jtb", token_gram, sketched, preferred_element_type=jnp.float32
    ).astype(jnp.bfloat16)
    block_gram = jnp.einsum("jtb,ktc->jbkc", sketched, weighted, preferred_element_type=jnp.float32)
    own_cols = own_blocks * width
    block_gram = block_gram.reshape(own_cols, own_cols)
    summed = lax.psum(block_gram, "dp")
    return summed / (lax.axis_size("dp") * tokens * model_width)


ALONG = pl.DeviceIdType.MESH
COUNT = 8
PIECES = 2 * COUNT
CUTS = 4
GB = 9
BELOW = tuple((i, j) for i in range(4) for j in range(i))
ROWS = tuple(128 if n < GB - 1 else 16 for n in range(GB))
UNITS = COUNT * (COUNT + 1) // 2
ORDER = tuple((1, COUNT - 1) if k == PIECES - 1 else (0, (k + 1) // 2) if k % 2 or k == 0 else (1, k // 2 - 1) for k in range(PIECES))
WHOLE = tuple((j, 0, BLK) for j in range(COUNT))
SPLIT = WHOLE[:-1] + ((COUNT - 1, 0, BLK // 2), (COUNT - 1, BLK // 2, BLK))
CHUNKS = (WHOLE, SPLIT)
STEPS = tuple((t, c, k) for k, (t, j) in enumerate(ORDER) for c, chunk in enumerate(CHUNKS[t]) if chunk[0] == j)


def units_of(chunk):
    j, lo, hi = chunk
    first = j * (j + 1) // 2
    if j < COUNT - 1:
        return first, j + 1
    half = COUNT // 2
    return first + half * (lo // (BLK // 2)), half * ((hi - lo) // (BLK // 2))


def mix_kernel(
    shards, parts, own, per, act_hbm, grads_hbm, bits_hbm, ids_hbm, got,
    act, grads, bits, flips, ids, rx, tx, grx, gtx, part, pairs, diagonals, full, sketch, keep, give, prx, rtx, rrx, gathered,
    l_sem, o_sem, z_send, z_recv, p_send, p_recv, r_send, r_recv, f_send, f_recv, a_send, a_recv, w_send, w_recv,
):
    z = lax.axis_index("shard")
    d = lax.axis_index("dp")
    core = lax.rem(d, 2)
    chip = d // 2
    last = shards - 1
    edge = (z == 0) | (z == last)
    middle = jnp.logical_not(edge)
    tokens = act.shape[0]
    width = BLK
    inv_block = 1.0 / math.sqrt(width)
    inv_shard = 1.0 / math.sqrt(shards)
    quarter = width // CUTS
    most = len(CHUNKS[1])

    barrier = pltpu.get_barrier_semaphore()

    def peer(m):
        flipped = 1 - lax.rem(chip, 2) if m & 1 else lax.rem(chip, 2)
        high = 1 - chip // 2 if m & 2 else chip // 2
        return (high * 2 + flipped) * 2 + core

    partner = chip * 2 + 1 - core
    for m in (1, 2, 3):
        pl.semaphore_signal(barrier, inc=1, device_id={"dp": peer(m)}, device_id_type=ALONG)
    pl.semaphore_signal(barrier, inc=1, device_id={"dp": partner}, device_id_type=ALONG)

    @pl.when(z > 0)
    def _():
        pl.semaphore_signal(barrier, inc=1, device_id={"shard": z - 1}, device_id_type=ALONG)

    @pl.when(z < last)
    def _():
        pl.semaphore_signal(barrier, inc=1, device_id={"shard": z + 1}, device_id_type=ALONG)

    loads = (
        pltpu.make_async_copy(act_hbm, act, l_sem.at[0]),
        pltpu.make_async_copy(ids_hbm, ids, l_sem.at[1]),
        pltpu.make_async_copy(bits_hbm, bits, l_sem.at[2]),
    ) + tuple(
        pltpu.make_async_copy(grads_hbm.at[:, pl.ds(width * b, width)], grads.at[b], l_sem.at[3]) for b in range(per)
    )
    for load in loads:
        load.start()

    row = lax.broadcasted_iota(jnp.int32, (width, width), 0)
    col = lax.broadcasted_iota(jnp.int32, (width, width), 1)
    both = row & col
    count = both & 1
    for level in range(1, width.bit_length() - 1):
        count = count + ((both >> level) & 1)
    table = (1 - 2 * (count & 1)).astype(jnp.float32)

    def contribution(owner, j):
        block = ids[owner, j]
        r = lax.div(block, per)
        local = block - r * per
        common = r & z
        odd = common & 1
        for level in range(1, shards.bit_length() - 1):
            odd = odd + ((common >> level) & 1)
        sign = 1 - 2 * (odd & 1)
        signs = flips[local] * sign.astype(jnp.float32)
        lm = lax.dot_general(
            (table * signs).astype(jnp.bfloat16), grads[local], (((1,), (1,)), ((), ())),
            preferred_element_type=jnp.float32)
        return ((lm * inv_block).astype(jnp.bfloat16).astype(jnp.float32) * inv_shard).astype(jnp.bfloat16)

    def owner_of(way, t):
        return jnp.where(way == 0, 1 - t, 2 + t)

    def piece(k):
        if isinstance(k, int):
            return ORDER[k]
        odd = lax.rem(k, 2) == 1
        final = k == PIECES - 1
        t = jnp.where(final | jnp.logical_not(odd | (k == 0)), 1, 0)
        j = jnp.where(final, COUNT - 1, jnp.where(t == 1, k // 2 - 1, (k + 1) // 2))
        return t, j

    def target(way):
        return jnp.where(way == 0, z - 1, z + 1)

    def s_move(way, k, h, who):
        rows = pl.ds(quarter * h, quarter)
        n = GB + CUTS * k + h
        return pltpu.make_async_remote_copy(
            tx.at[way, k, rows], rx.at[way, k, rows], z_send.at[way, 1], z_recv.at[way, n],
            device_id={"shard": who}, device_id_type=ALONG)

    def s_copy(way, k, h):
        return s_move(way, k, h, target(way))

    def g_move(way, n, who):
        rows = pl.ds(0, ROWS[n])
        return pltpu.make_async_remote_copy(
            gtx.at[way, n, rows], grx.at[way, n, rows], z_send.at[way, 2 * (n // (GB - 1))], z_recv.at[way, n],
            device_id={"shard": who}, device_id_type=ALONG)

    def g_copy(way, n):
        return g_move(way, n, target(way))

    def z_sent(way):
        pltpu.make_async_remote_copy(
            gtx.at[way, 0 : GB - 1], grx.at[way, 0 : GB - 1], z_send.at[way, 0], z_recv.at[way, 0],
            device_id={"shard": target(way)}, device_id_type=ALONG).wait_send()
        g_copy(way, GB - 1).wait_send()
        pltpu.make_async_remote_copy(
            tx.at[way], rx.at[way], z_send.at[way, 1], z_recv.at[way, 0],
            device_id={"shard": target(way)}, device_id_type=ALONG).wait_send()

    def square(i, j):
        return part[128 * i : 128 * (i + 1), 128 * j : 128 * (j + 1)]

    def gpart(n):
        if n < len(BELOW):
            return square(*BELOW[n])
        if n < GB - 1:
            return pairs[n - len(BELOW)]
        return diagonals[...]

    def gsum(way, n):
        return (grx[way, n, : ROWS[n]].astype(jnp.float32) + gpart(n)).astype(jnp.bfloat16)

    def fill(way, k):
        t, j = piece(k)
        tx[way, k] = contribution(owner_of(way, t), j)

    def units(t, c):
        return pl.ds(*units_of(CHUNKS[t][c]))

    def late(t, c):
        return int(CHUNKS[t][c][0] >= COUNT - 2)

    def a_copy(t, c, slot, who):
        arrival = a_recv.at[most + late(t, c)] if slot == 3 else a_recv.at[c]
        return pltpu.make_async_remote_copy(
            gathered.at[d, units(t, c)], gathered.at[d, units(t, c)], a_send.at[slot], arrival,
            device_id={"dp": who}, device_id_type=ALONG)

    def w_copy(t, c, m):
        return pltpu.make_async_remote_copy(
            gathered.at[peer(m), units(t, c)], gathered.at[peer(m), units(t, c)],
            w_send.at[0], w_recv.at[late(t, c)],
            device_id={"dp": partner}, device_id_type=ALONG)

    def spread(t, c):
        for m in (1, 2, 3):
            a_copy(t, c, m - 1, peer(m)).start()
        a_copy(t, c, 3, partner).start()

    def relay(t, c):
        us = units(t, c)
        pltpu.make_async_remote_copy(
            gathered.at[0:3, us], gathered.at[0:3, us], a_send.at[0], a_recv.at[c],
            device_id={"dp": partner}, device_id_type=ALONG).wait_recv()
        for m in (1, 2, 3):
            w_copy(t, c, m).start()

    early = (COUNT - 2) * (COUNT - 1) // 2
    GROUPS = ((0, early), (early, UNITS))

    def leave(g):
        us = pl.ds(GROUPS[g][0], GROUPS[g][1] - GROUPS[g][0])
        return pltpu.make_async_copy(gathered.at[:, us], got.at[:, us], o_sem.at[g])

    def settle(g):
        us = pl.ds(GROUPS[g][0], GROUPS[g][1] - GROUPS[g][0])
        pltpu.make_async_remote_copy(
            gathered.at[0, us], gathered.at[0, us], a_send.at[3], a_recv.at[most + g],
            device_id={"dp": partner}, device_id_type=ALONG).wait_recv()
        pltpu.make_async_remote_copy(
            gathered.at[0:3, us], gathered.at[0:3, us], w_send.at[0], w_recv.at[g],
            device_id={"dp": partner}, device_id_type=ALONG).wait_recv()
        leave(g).start()

    def finish():
        for slot in range(4):
            pltpu.make_async_remote_copy(
                gathered.at[0], gathered.at[0], a_send.at[slot], a_recv.at[0],
                device_id={"dp": partner}, device_id_type=ALONG).wait_send()
        pltpu.make_async_remote_copy(
            gathered.at[0:3], gathered.at[0:3], w_send.at[0], w_recv.at[0],
            device_id={"dp": partner}, device_id_type=ALONG).wait_send()
        for g in range(2):
            leave(g).wait()

    def f_copy(c, who):
        us = units(0, c)
        return pltpu.make_async_remote_copy(
            rrx.at[3, us], gathered.at[d, us], f_send.at[0], f_recv.at[c],
            device_id={"shard": who}, device_id_type=ALONG)

    loads[0].wait()
    part[...] = lax.dot_general(act[...], act[...], (((1,), (1,)), ((), ())), preferred_element_type=jnp.float32)
    diagonals[...] = jnp.zeros_like(diagonals)
    for n in range(2):
        second = square(2 * n + 1, 2 * n + 1)
        pairs[n] = jnp.where(row >= col, square(2 * n, 2 * n), second)
        diagonals[n : n + 1] = jnp.sum(jnp.where(row == col, second, 0.0), axis=0, keepdims=True)
    def loaded():
        loads[1].wait()
        loads[2].wait()
        pltpu.make_async_copy(grads, grads, l_sem.at[3]).wait()
        for b in range(per):
            flips[b] = (1 - 2 * bits[width * b : width * (b + 1)].reshape(1, width)).astype(jnp.float32)

    @pl.when(edge)
    def _():
        pl.semaphore_wait(barrier, 5)

    @pl.when(middle)
    def _():
        pl.semaphore_wait(barrier, 6)

    @pl.when(edge)
    def _():
        out_way = jnp.where(z == 0, 1, 0)
        in_way = 1 - out_way
        side = target(out_way)
        for n in range(GB):
            gtx[out_way, n, : ROWS[n]] = gpart(n).astype(jnp.bfloat16)
            g_copy(out_way, n).start()
        loaded()

        def push(k, carry):
            fill(out_way, k)
            for h in range(CUTS):
                s_copy(out_way, k, h).start()
            return carry

        lax.fori_loop(0, PIECES, push, 0)

        def ready(p, carry):
            t, j = p // COUNT, lax.rem(p, COUNT)
            sketch[t, pl.ds(pl.multiple_of(width * j, width), width)] = contribution(owner_of(in_way, t), j)
            return carry

        lax.fori_loop(0, PIECES, ready, 0)

        for n in range(GB):
            g_move(in_way, n, side).wait_recv()
            if n < len(BELOW):
                r, c = BELOW[n]
                block = gsum(in_way, n)
                full[128 * r : 128 * (r + 1), 128 * c : 128 * (c + 1)] = block
                full[128 * c : 128 * (c + 1), 128 * r : 128 * (r + 1)] = block.T
        ends = gsum(in_way, GB - 1).astype(jnp.float32)
        for n in range(2):
            both_of = gsum(in_way, len(BELOW) + n).astype(jnp.float32)
            turned = both_of.T
            first = jnp.where(row >= col, both_of, turned)
            second = jnp.where(row < col, both_of, jnp.where(row > col, turned, ends[n : n + 1]))
            for i, block in ((2 * n, first), (2 * n + 1, second)):
                full[128 * i : 128 * (i + 1), 128 * i : 128 * (i + 1)] = block.astype(jnp.bfloat16)

        def where(q):
            t, c, k = STEPS[q]
            first, number = units_of(CHUNKS[t][c])
            return t, c, k, pl.ds(UNITS * t + first, number)

        def p_copy(q):
            t, c, k, us = where(q)
            return pltpu.make_async_remote_copy(
                give.at[us], prx.at[us], p_send.at[0], p_recv.at[q],
                device_id={"dp": partner}, device_id_type=ALONG)

        def r_copy(q, m):
            t, c, k, us = where(q)
            return pltpu.make_async_remote_copy(
                rtx.at[peer(m) // 2, us], rrx.at[m - 1, us], r_send.at[m - 1], r_recv.at[q],
                device_id={"dp": peer(m)}, device_id_type=ALONG)

        def step_a(q, between=None):
            t, c, k, us = where(q)
            j, lo, hi = CHUNKS[t][c]
            for h in range(lo // quarter, hi // quarter):
                if between is not None and h == CUTS - 1:
                    step_c(between)
                s_move(in_way, k, h, side).wait_recv()
                rows = slice(width * j + quarter * h, width * j + quarter * (h + 1))
                arrived = rx[in_way, k, quarter * h : quarter * (h + 1)].astype(jnp.float32)
                sketch[t, rows] = (arrived + sketch[t, rows].astype(jnp.float32)).astype(jnp.bfloat16)
            mine = sketch[t, width * j + lo : width * j + hi]
            weighted = jnp.dot(mine, full[...], preferred_element_type=jnp.float32).astype(jnp.bfloat16)
            half = width // 2
            first, number = units_of(CHUNKS[t][c])

            def put(u, top, bottom):
                keep[UNITS * t + u] = jnp.where(core == 0, top, bottom)
                give[UNITS * t + u] = jnp.where(core == 0, bottom, top).astype(jnp.bfloat16)

            for i in range(0, j + 1, 2):
                end = min(i + 2, j + 1)
                block = lax.dot_general(
                    weighted, sketch[t, width * i : width * end], (((1,), (1,)), ((), ())),
                    preferred_element_type=jnp.float32)
                if j < COUNT - 1:
                    for n in range(i, end):
                        cols = slice(width * (n - i), width * (n - i + 1))
                        put(first + n, block[:half, cols], block[half:, cols])
                else:
                    for g in range((hi - lo) // half):
                        rows = slice(half * g, half * (g + 1))
                        put(first + COUNT // 2 * g + i // 2, block[rows, :width], block[rows, width:])
            p_copy(q).start()

        def step_b(q):
            t, c, k, us = where(q)
            p_copy(q).wait_recv()
            total = (keep[us] + prx[us].astype(jnp.float32)).astype(jnp.bfloat16)
            for n in range(4):
                rtx[n, us] = total[:, 16 * n : 16 * (n + 1)]
            for m in (1, 2, 3):
                r_copy(q, m).start()

        def step_c(q):
            t, c, k, us = where(q)
            pltpu.make_async_remote_copy(
                rrx.at[0:3, us], rrx.at[0:3, us], r_send.at[0], r_recv.at[q],
                device_id={"dp": partner}, device_id_type=ALONG).wait_recv()
            total = rtx[chip, us].astype(jnp.float32)
            for m in range(3):
                total = total + rrx[m, us].astype(jnp.float32)
            total = (total * (1.0 / (parts * tokens * act.shape[1] * shards))).astype(jnp.bfloat16)
            if t == 0:
                rrx[3, units(t, c)] = total
                f_copy(c, side).start()
            else:
                gathered[d, units(t, c)] = total
                spread(t, c)

        def step_d(q):
            t, c, k, us = where(q)
            if t == 1:
                relay(t, c)

        def drain():
            pltpu.make_async_remote_copy(
                give, prx, p_send.at[0], p_recv.at[0],
                device_id={"dp": partner}, device_id_type=ALONG).wait_send()
            for m in range(3):
                pltpu.make_async_remote_copy(
                    rtx.at[m], rrx.at[m], r_send.at[m], r_recv.at[0],
                    device_id={"dp": partner}, device_id_type=ALONG).wait_send()
            us = pl.ds(0, UNITS)
            pltpu.make_async_remote_copy(
                rrx.at[3, us], gathered.at[d, us], f_send.at[0], f_recv.at[0],
                device_id={"shard": side}, device_id_type=ALONG).wait_send()
            z_sent(out_way)

        steps = len(STEPS)
        for q in range(steps - 3):
            step_a(q, q - 2 if q >= 2 else None)
            step_b(q)
            if q >= 4:
                step_d(q - 4)
        e = steps - 3
        step_a(e, e - 2)
        step_a(e + 1)
        step_b(e)
        step_a(e + 2)
        step_b(e + 1)
        step_c(e - 1)
        step_b(e + 2)
        step_d(e - 4)
        step_d(e - 3)
        step_d(e - 2)
        step_c(e)
        step_c(e + 1)
        step_c(e + 2)
        step_d(e - 1)
        step_d(e)
        step_d(e + 1)
        drain()
        settle(0)
        step_d(e + 2)
        settle(1)
        finish()

    @pl.when(middle)
    def _():
        near = jnp.where(z == 1, 1, 0)
        far = 1 - near
        outward = jnp.where(z == 1, 0, last)
        loaded()

        def pass_g(way, n):
            g_copy(way, n).wait_recv()
            gtx[way, n, : ROWS[n]] = gsum(way, n)
            g_copy(way, n).start()

        def pass_s(way, k, h):
            s_copy(way, k, h).wait_recv()
            rows = slice(quarter * h, quarter * (h + 1))
            tx[way, k, rows] = (rx[way, k, rows].astype(jnp.float32) + tx[way, k, rows].astype(jnp.float32)).astype(jnp.bfloat16)
            s_copy(way, k, h).start()

        lag = CUTS + 1
        for n in range(GB):
            pass_g(near, n)
            if n >= lag:
                pass_g(far, n - lag)
        fill(near, 0)
        for h in range(CUTS):
            pass_s(near, 0, h)
            pass_g(far, GB - lag + h)
        fill(near, 1)
        fill(far, 0)
        pass_s(near, 1, 0)
        pass_g(far, GB - 1)
        for h in range(1, CUTS):
            pass_s(near, 1, h)
            pass_s(far, 0, h - 1)

        def both_ways(k, carry):
            fill(near, k)
            fill(far, k - 1)
            pass_s(near, k, 0)
            pass_s(far, k - 2, CUTS - 1)
            for h in range(1, CUTS):
                pass_s(near, k, h)
                pass_s(far, k - 1, h - 1)
            return carry

        lax.fori_loop(2, PIECES, both_ways, 0)
        fill(far, PIECES - 1)
        pass_s(far, PIECES - 2, CUTS - 1)
        for h in range(CUTS):
            pass_s(far, PIECES - 1, h)

        chunks = len(CHUNKS[0])
        for c in range(chunks):
            f_copy(c, outward).wait_recv()
            spread(0, c)
            if c >= 2:
                relay(0, c - 2)
        z_sent(near)
        z_sent(far)
        relay(0, chunks - 2)
        settle(0)
        relay(0, chunks - 1)
        settle(1)
        finish()


def assemble_kernel(source, out, got, held, sems):
    load = pltpu.make_async_copy(source, got, sems.at[COUNT])
    load.start()
    load.wait()
    half = BLK // 2

    def unit(u):
        rows = [got[2 * n + h, u] for h in range(2) for n in range(4)]
        return jnp.concatenate(rows, axis=0).astype(jnp.float32)

    def put(i):
        rows = pl.ds(BLK * i, BLK)
        return pltpu.make_async_copy(held.at[rows], out.at[rows], sems.at[i])

    final = COUNT - 1
    first = final * COUNT // 2
    lower = {}
    for v in range(COUNT // 2):
        top, bottom = unit(first + v), unit(first + COUNT // 2 + v)
        for g in range(2):
            rows = slice(half * g, half * (g + 1))
            lower[2 * v + g] = jnp.concatenate([top[rows], bottom[rows]], axis=0)
    square = lower[final]
    row = lax.broadcasted_iota(jnp.int32, (BLK, BLK), 0)
    col = lax.broadcasted_iota(jnp.int32, (BLK, BLK), 1)
    lower[final] = jnp.where((row < half) & (col >= half), square.T, square)
    for i in range(COUNT):
        for j in range(COUNT):
            if i == final:
                block = lower[j]
            elif j == final:
                block = lower[i].T
            elif j <= i:
                block = unit(i * (i + 1) // 2 + j)
            else:
                block = unit(j * (j + 1) // 2 + i).T
            held[BLK * i : BLK * (i + 1), BLK * j : BLK * (j + 1)] = block
        put(i).start()
    for i in range(COUNT):
        put(i).wait()


def fast_body(shards, parts, activations, out_grads, sign_bits, block_ids):
    tokens, columns = out_grads.shape
    per = columns // BLK
    own = block_ids.shape[1]
    hbm = pl.BlockSpec(memory_space=pltpu.HBM)
    bf, f32 = jnp.bfloat16, jnp.float32
    dma = pltpu.SemaphoreType.DMA
    steps, most = len(STEPS), len(CHUNKS[1])
    got = pl.pallas_call(
        functools.partial(mix_kernel, shards, parts, own, per),
        out_shape=jax.ShapeDtypeStruct((parts, UNITS, 16, BLK), bf),
        in_specs=[hbm, hbm, hbm, hbm],
        out_specs=hbm,
        scratch_shapes=[
            pltpu.VMEM(activations.shape, bf),
            pltpu.VMEM((per, tokens, BLK), bf),
            pltpu.VMEM(sign_bits.shape, jnp.int32),
            pltpu.VMEM((per, 1, BLK), f32),
            pltpu.SMEM(block_ids.shape, jnp.int32),
            pltpu.VMEM((2, PIECES, BLK, tokens), bf),
            pltpu.VMEM((2, PIECES, BLK, tokens), bf),
            pltpu.VMEM((2, GB, 128, 128), bf),
            pltpu.VMEM((2, GB, 128, 128), bf),
            pltpu.VMEM((tokens, tokens), f32),
            pltpu.VMEM((2, 128, 128), f32),
            pltpu.VMEM((16, 128), f32),
            pltpu.VMEM((tokens, tokens), bf),
            pltpu.VMEM((2, own * BLK, tokens), bf),
            pltpu.VMEM((2 * UNITS, 64, BLK), f32),
            pltpu.VMEM((2 * UNITS, 64, BLK), bf),
            pltpu.VMEM((2 * UNITS, 64, BLK), bf),
            pltpu.VMEM((4, 2 * UNITS, 16, BLK), bf),
            pltpu.VMEM((4, 2 * UNITS, 16, BLK), bf),
            pltpu.VMEM((parts, UNITS, 16, BLK), bf),
            dma((4,)), dma((2,)),
            dma((2, 3)), dma((2, GB + CUTS * PIECES)),
            dma((1,)), dma((steps,)),
            dma((3,)), dma((steps,)),
            dma((1,)), dma((COUNT,)),
            dma((4,)), dma((most + 2,)),
            dma((1,)), dma((2,)),
        ],
        compiler_params=pltpu.CompilerParams(collective_id=0, has_side_effects=True, vmem_limit_bytes=int(62.5 * 2**20)),
        name="mix",
    )(activations, out_grads, sign_bits, block_ids)
    return pl.pallas_call(
        assemble_kernel,
        out_shape=jax.ShapeDtypeStruct((own * BLK, own * BLK), f32),
        in_specs=[hbm],
        out_specs=hbm,
        scratch_shapes=[
            pltpu.VMEM((parts, UNITS, 16, BLK), bf), pltpu.VMEM((own * BLK, own * BLK), f32), dma((own + 1,))],
        compiler_params=pltpu.CompilerParams(vmem_limit_bytes=int(62.5 * 2**20)),
        name="assemble",
    )(got)


def solution(mesh):
    in_specs = (P("dp", "shard"), P("dp", "shard"), P("shard"), P())
    out_specs = P("shard", None)
    shards, parts = mesh.shape["shard"], mesh.shape["dp"]
    chosen = functools.partial(fast_body, shards, parts) if (shards, parts) == (4, 8) else body
    return jax.shard_map(chosen, mesh=mesh, in_specs=in_specs, out_specs=out_specs, check_vma=False)
```

```python
import functools
import math

import jax
import jax.numpy as jnp
from jax import lax
from jax.experimental import pallas as pl
from jax.experimental.pallas import tpu as pltpu
from jax.sharding import PartitionSpec as P

BLK = 128
CAP = 2


def partner_2(x, axis, distance):
    return lax.ppermute(x, axis, [(i, i ^ 1 << distance) for i in range(lax.axis_size(axis))])


def parity_table(count):
    index = jnp.arange(count, dtype=jnp.int32)
    total = jnp.zeros((count, count), jnp.int32)
    for level in range(count.bit_length() - 1):
        total = total + (
            jnp.right_shift(index[:, None], level) & jnp.right_shift(index[None, :], level) & 1
        )
    return (1 - 2 * (total % 2)).astype(jnp.float32)


def route_sampled(mixed, block_ids, me_index, shards, blocks_per, tokens, width):
    groups = block_ids.shape[1] // CAP
    sources = block_ids[:, ::CAP] // blocks_per
    local_ids = (block_ids % blocks_per).reshape(shards, groups, CAP)
    matched = sources == me_index
    chosen = jnp.sum(jnp.where(matched[:, :, None], local_ids, 0), axis=1)
    live_rows = jnp.any(matched, axis=1).astype(jnp.bfloat16)
    outgoing = jnp.take(mixed, chosen.reshape(-1), axis=0).reshape(shards, CAP, tokens, width)
    return (outgoing * live_rows[:, None, None, None], jnp.take(sources, me_index, axis=0))


def body(activations, out_grads, sign_bits, block_ids):
    shards = lax.axis_size("shard")
    me_index = lax.axis_index("shard")
    tokens = out_grads.shape[0]
    width = BLK
    own_blocks = block_ids.shape[1]
    blocks_per = out_grads.shape[1] // width
    model_width = activations.shape[1] * shards
    inv_block = 1.0 / math.sqrt(width)
    inv_shard = 1.0 / math.sqrt(shards)
    partial_gram = jnp.dot(activations, activations.T, preferred_element_type=jnp.float32)
    token_gram = lax.psum(partial_gram, "shard").astype(jnp.bfloat16)
    sign_values = (1 - 2 * sign_bits).astype(jnp.bfloat16)
    flipped = (out_grads * sign_values[None, :]).reshape(tokens, blocks_per, width)
    block_table = parity_table(width).astype(jnp.bfloat16)
    local_mix = jnp.einsum("tbj,jk->btk", flipped, block_table, preferred_element_type=jnp.float32)
    local_mix = (local_mix * inv_block).astype(jnp.bfloat16)
    running = local_mix.astype(jnp.float32)
    for level in range(shards.bit_length() - 1):
        partner = partner_2(running, "shard", level)
        upper = jnp.right_shift(me_index, level) & 1 == 1
        running = jnp.where(upper, partner - running, running + partner)
    mixed = (running * inv_shard).astype(jnp.bfloat16)
    outgoing, own_sources = route_sampled(
        mixed, block_ids, me_index, shards, blocks_per, tokens, width
    )
    incoming = lax.all_to_all(outgoing, "shard", split_axis=0, concat_axis=0, tiled=True)
    sketched = jnp.take(incoming, own_sources, axis=0).reshape(own_blocks, tokens, width)
    weighted = jnp.einsum(
        "tu,jub->jtb", token_gram, sketched, preferred_element_type=jnp.float32
    ).astype(jnp.bfloat16)
    block_gram = jnp.einsum("jtb,ktc->jbkc", sketched, weighted, preferred_element_type=jnp.float32)
    own_cols = own_blocks * width
    block_gram = block_gram.reshape(own_cols, own_cols)
    summed = lax.psum(block_gram, "dp")
    return summed / (lax.axis_size("dp") * tokens * model_width)


ALONG = pl.DeviceIdType.MESH
COUNT = 8
PIECES = 2 * COUNT
CUTS = 4
GB = 9
BELOW = tuple((i, j) for i in range(4) for j in range(i))
ROWS = tuple(128 if n < GB - 1 else 16 for n in range(GB))
UNITS = COUNT * (COUNT + 1) // 2
ORDER = tuple((1, COUNT - 1) if k == PIECES - 1 else (0, (k + 1) // 2) if k % 2 or k == 0 else (1, k // 2 - 1) for k in range(PIECES))
WHOLE = tuple((j, 0, BLK) for j in range(COUNT))
SPLIT = WHOLE[:-1] + ((COUNT - 1, 0, BLK // 2), (COUNT - 1, BLK // 2, BLK))
CHUNKS = (WHOLE, SPLIT)
STEPS = tuple((t, c, k) for k, (t, j) in enumerate(ORDER) for c, chunk in enumerate(CHUNKS[t]) if chunk[0] == j)


def units_of(chunk):
    j, lo, hi = chunk
    first = j * (j + 1) // 2
    if j < COUNT - 1:
        return first, j + 1
    half = COUNT // 2
    return first + half * (lo // (BLK // 2)), half * ((hi - lo) // (BLK // 2))


def mix_kernel(
    shards, parts, own, per, act_hbm, grads_hbm, bits_hbm, ids_hbm, got,
    act, grads, bits, flips, ids, rx, tx, grx, gtx, part, pairs, diagonals, full, sketch, keep, give, prx, rtx, rrx, gathered,
    l_sem, o_sem, z_send, z_recv, p_send, p_recv, r_send, r_recv, f_send, f_recv, a_send, a_recv, w_send, w_recv,
):
    z = lax.axis_index("shard")
    d = lax.axis_index("dp")
    core = lax.rem(d, 2)
    chip = d // 2
    last = shards - 1
    edge = (z == 0) | (z == last)
    middle = jnp.logical_not(edge)
    tokens = act.shape[0]
    width = BLK
    inv_block = 1.0 / math.sqrt(width)
    inv_shard = 1.0 / math.sqrt(shards)
    quarter = width // CUTS
    most = len(CHUNKS[1])

    barrier = pltpu.get_barrier_semaphore()

    def peer(m):
        flipped = 1 - lax.rem(chip, 2) if m & 1 else lax.rem(chip, 2)
        high = 1 - chip // 2 if m & 2 else chip // 2
        return (high * 2 + flipped) * 2 + core

    partner = chip * 2 + 1 - core
    for m in (1, 2, 3):
        pl.semaphore_signal(barrier, inc=1, device_id={"dp": peer(m)}, device_id_type=ALONG)
    pl.semaphore_signal(barrier, inc=1, device_id={"dp": partner}, device_id_type=ALONG)

    @pl.when(z > 0)
    def _():
        pl.semaphore_signal(barrier, inc=1, device_id={"shard": z - 1}, device_id_type=ALONG)

    @pl.when(z < last)
    def _():
        pl.semaphore_signal(barrier, inc=1, device_id={"shard": z + 1}, device_id_type=ALONG)

    loads = (
        pltpu.make_async_copy(act_hbm, act, l_sem.at[0]),
        pltpu.make_async_copy(ids_hbm, ids, l_sem.at[1]),
        pltpu.make_async_copy(bits_hbm, bits, l_sem.at[2]),
    ) + tuple(
        pltpu.make_async_copy(grads_hbm.at[:, pl.ds(width * b, width)], grads.at[b], l_sem.at[3]) for b in range(per)
    )
    for load in loads:
        load.start()

    row = lax.broadcasted_iota(jnp.int32, (width, width), 0)
    col = lax.broadcasted_iota(jnp.int32, (width, width), 1)
    both = row & col
    count = both & 1
    for level in range(1, width.bit_length() - 1):
        count = count + ((both >> level) & 1)
    table = (1 - 2 * (count & 1)).astype(jnp.float32)

    def contribution(owner, j):
        block = ids[owner, j]
        r = lax.div(block, per)
        local = block - r * per
        common = r & z
        odd = common & 1
        for level in range(1, shards.bit_length() - 1):
            odd = odd + ((common >> level) & 1)
        sign = 1 - 2 * (odd & 1)
        signs = flips[local] * sign.astype(jnp.float32)
        lm = lax.dot_general(
            (table * signs).astype(jnp.bfloat16), grads[local], (((1,), (1,)), ((), ())),
            preferred_element_type=jnp.float32)
        return ((lm * inv_block).astype(jnp.bfloat16).astype(jnp.float32) * inv_shard).astype(jnp.bfloat16)

    def owner_of(way, t):
        return jnp.where(way == 0, 1 - t, 2 + t)

    def piece(k):
        if isinstance(k, int):
            return ORDER[k]
        odd = lax.rem(k, 2) == 1
        final = k == PIECES - 1
        t = jnp.where(final | jnp.logical_not(odd | (k == 0)), 1, 0)
        j = jnp.where(final, COUNT - 1, jnp.where(t == 1, k // 2 - 1, (k + 1) // 2))
        return t, j

    def target(way):
        return jnp.where(way == 0, z - 1, z + 1)

    def s_move(way, k, h, who):
        rows = pl.ds(quarter * h, quarter)
        n = GB + CUTS * k + h
        return pltpu.make_async_remote_copy(
            tx.at[way, k, rows], rx.at[way, k, rows], z_send.at[way, 1], z_recv.at[way, n],
            device_id={"shard": who}, device_id_type=ALONG)

    def s_copy(way, k, h):
        return s_move(way, k, h, target(way))

    def g_move(way, n, who):
        rows = pl.ds(0, ROWS[n])
        return pltpu.make_async_remote_copy(
            gtx.at[way, n, rows], grx.at[way, n, rows], z_send.at[way, 2 * (n // (GB - 1))], z_recv.at[way, n],
            device_id={"shard": who}, device_id_type=ALONG)

    def g_copy(way, n):
        return g_move(way, n, target(way))

    def z_sent(way):
        pltpu.make_async_remote_copy(
            gtx.at[way, 0 : GB - 1], grx.at[way, 0 : GB - 1], z_send.at[way, 0], z_recv.at[way, 0],
            device_id={"shard": target(way)}, device_id_type=ALONG).wait_send()
        g_copy(way, GB - 1).wait_send()
        pltpu.make_async_remote_copy(
            tx.at[way], rx.at[way], z_send.at[way, 1], z_recv.at[way, 0],
            device_id={"shard": target(way)}, device_id_type=ALONG).wait_send()

    def square(i, j):
        return part[128 * i : 128 * (i + 1), 128 * j : 128 * (j + 1)]

    def gpart(n):
        if n < len(BELOW):
            return square(*BELOW[n])
        if n < GB - 1:
            return pairs[n - len(BELOW)]
        return diagonals[...]

    def gsum(way, n):
        return (grx[way, n, : ROWS[n]].astype(jnp.float32) + gpart(n)).astype(jnp.bfloat16)

    def fill(way, k):
        t, j = piece(k)
        tx[way, k] = contribution(owner_of(way, t), j)

    def units(t, c):
        return pl.ds(*units_of(CHUNKS[t][c]))

    def late(t, c):
        return int(CHUNKS[t][c][0] >= COUNT - 2)

    def a_copy(t, c, slot, who):
        arrival = a_recv.at[most + late(t, c)] if slot == 3 else a_recv.at[c]
        return pltpu.make_async_remote_copy(
            gathered.at[d, units(t, c)], gathered.at[d, units(t, c)], a_send.at[slot], arrival,
            device_id={"dp": who}, device_id_type=ALONG)

    def w_copy(t, c, m):
        return pltpu.make_async_remote_copy(
            gathered.at[peer(m), units(t, c)], gathered.at[peer(m), units(t, c)],
            w_send.at[0], w_recv.at[late(t, c)],
            device_id={"dp": partner}, device_id_type=ALONG)

    def spread(t, c):
        for m in (1, 2, 3):
            a_copy(t, c, m - 1, peer(m)).start()
        a_copy(t, c, 3, partner).start()

    def relay(t, c):
        us = units(t, c)
        pltpu.make_async_remote_copy(
            gathered.at[0:3, us], gathered.at[0:3, us], a_send.at[0], a_recv.at[c],
            device_id={"dp": partner}, device_id_type=ALONG).wait_recv()
        for m in (1, 2, 3):
            w_copy(t, c, m).start()

    early = (COUNT - 2) * (COUNT - 1) // 2
    GROUPS = ((0, early), (early, UNITS))

    def leave(g):
        us = pl.ds(GROUPS[g][0], GROUPS[g][1] - GROUPS[g][0])
        return pltpu.make_async_copy(gathered.at[:, us], got.at[:, us], o_sem.at[g])

    def settle(g):
        us = pl.ds(GROUPS[g][0], GROUPS[g][1] - GROUPS[g][0])
        pltpu.make_async_remote_copy(
            gathered.at[0, us], gathered.at[0, us], a_send.at[3], a_recv.at[most + g],
            device_id={"dp": partner}, device_id_type=ALONG).wait_recv()
        pltpu.make_async_remote_copy(
            gathered.at[0:3, us], gathered.at[0:3, us], w_send.at[0], w_recv.at[g],
            device_id={"dp": partner}, device_id_type=ALONG).wait_recv()
        leave(g).start()

    def finish():
        for slot in range(4):
            pltpu.make_async_remote_copy(
                gathered.at[0], gathered.at[0], a_send.at[slot], a_recv.at[0],
                device_id={"dp": partner}, device_id_type=ALONG).wait_send()
        pltpu.make_async_remote_copy(
            gathered.at[0:3], gathered.at[0:3], w_send.at[0], w_recv.at[0],
            device_id={"dp": partner}, device_id_type=ALONG).wait_send()
        for g in range(2):
            leave(g).wait()

    def f_copy(c, who):
        us = units(0, c)
        return pltpu.make_async_remote_copy(
            rrx.at[3, us], gathered.at[d, us], f_send.at[0], f_recv.at[c],
            device_id={"shard": who}, device_id_type=ALONG)

    loads[0].wait()
    part[...] = lax.dot_general(act[...], act[...], (((1,), (1,)), ((), ())), preferred_element_type=jnp.float32)
    diagonals[...] = jnp.zeros_like(diagonals)
    for n in range(2):
        second = square(2 * n + 1, 2 * n + 1)
        pairs[n] = jnp.where(row >= col, square(2 * n, 2 * n), second)
        diagonals[n : n + 1] = jnp.sum(jnp.where(row == col, second, 0.0), axis=0, keepdims=True)
    def loaded():
        loads[1].wait()
        loads[2].wait()
        pltpu.make_async_copy(grads, grads, l_sem.at[3]).wait()
        for b in range(per):
            flips[b] = (1 - 2 * bits[width * b : width * (b + 1)].reshape(1, width)).astype(jnp.float32)

    @pl.when(edge)
    def _():
        pl.semaphore_wait(barrier, 5)

    @pl.when(middle)
    def _():
        pl.semaphore_wait(barrier, 6)

    @pl.when(edge)
    def _():
        out_way = jnp.where(z == 0, 1, 0)
        in_way = 1 - out_way
        side = target(out_way)
        for n in range(GB):
            gtx[out_way, n, : ROWS[n]] = gpart(n).astype(jnp.bfloat16)
            g_copy(out_way, n).start()
        loaded()

        def push(k, carry):
            fill(out_way, k)
            for h in range(CUTS):
                s_copy(out_way, k, h).start()
            return carry

        lax.fori_loop(0, PIECES, push, 0)

        def ready(p, carry):
            t, j = p // COUNT, lax.rem(p, COUNT)
            sketch[t, pl.ds(pl.multiple_of(width * j, width), width)] = contribution(owner_of(in_way, t), j)
            return carry

        lax.fori_loop(0, PIECES, ready, 0)

        for n in range(GB):
            g_move(in_way, n, side).wait_recv()
            if n < len(BELOW):
                r, c = BELOW[n]
                block = gsum(in_way, n)
                full[128 * r : 128 * (r + 1), 128 * c : 128 * (c + 1)] = block
                full[128 * c : 128 * (c + 1), 128 * r : 128 * (r + 1)] = block.T
        ends = gsum(in_way, GB - 1).astype(jnp.float32)
        for n in range(2):
            both_of = gsum(in_way, len(BELOW) + n).astype(jnp.float32)
            turned = both_of.T
            first = jnp.where(row >= col, both_of, turned)
            second = jnp.where(row < col, both_of, jnp.where(row > col, turned, ends[n : n + 1]))
            for i, block in ((2 * n, first), (2 * n + 1, second)):
                full[128 * i : 128 * (i + 1), 128 * i : 128 * (i + 1)] = block.astype(jnp.bfloat16)

        def where(q):
            t, c, k = STEPS[q]
            first, number = units_of(CHUNKS[t][c])
            return t, c, k, pl.ds(UNITS * t + first, number)

        def p_copy(q):
            t, c, k, us = where(q)
            return pltpu.make_async_remote_copy(
                give.at[us], prx.at[us], p_send.at[0], p_recv.at[q],
                device_id={"dp": partner}, device_id_type=ALONG)

        def r_copy(q, m):
            t, c, k, us = where(q)
            return pltpu.make_async_remote_copy(
                rtx.at[peer(m) // 2, us], rrx.at[m - 1, us], r_send.at[m - 1], r_recv.at[q],
                device_id={"dp": peer(m)}, device_id_type=ALONG)

        def step_a(q, between=None):
            t, c, k, us = where(q)
            j, lo, hi = CHUNKS[t][c]
            for h in range(lo // quarter, hi // quarter):
                if between is not None and h == CUTS - 1:
                    step_c(between)
                s_move(in_way, k, h, side).wait_recv()
                rows = slice(width * j + quarter * h, width * j + quarter * (h + 1))
                arrived = rx[in_way, k, quarter * h : quarter * (h + 1)].astype(jnp.float32)
                sketch[t, rows] = (arrived + sketch[t, rows].astype(jnp.float32)).astype(jnp.bfloat16)
            mine = sketch[t, width * j + lo : width * j + hi]
            weighted = jnp.dot(mine, full[...], preferred_element_type=jnp.float32).astype(jnp.bfloat16)
            half = width // 2
            first, number = units_of(CHUNKS[t][c])

            def put(u, top, bottom):
                keep[UNITS * t + u] = jnp.where(core == 0, top, bottom)
                give[UNITS * t + u] = jnp.where(core == 0, bottom, top).astype(jnp.bfloat16)

            for i in range(0, j + 1, 2):
                end = min(i + 2, j + 1)
                block = lax.dot_general(
                    weighted, sketch[t, width * i : width * end], (((1,), (1,)), ((), ())),
                    preferred_element_type=jnp.float32)
                if j < COUNT - 1:
                    for n in range(i, end):
                        cols = slice(width * (n - i), width * (n - i + 1))
                        put(first + n, block[:half, cols], block[half:, cols])
                else:
                    for g in range((hi - lo) // half):
                        rows = slice(half * g, half * (g + 1))
                        put(first + COUNT // 2 * g + i // 2, block[rows, :width], block[rows, width:])
            p_copy(q).start()

        def step_b(q):
            t, c, k, us = where(q)
            p_copy(q).wait_recv()
            total = (keep[us] + prx[us].astype(jnp.float32)).astype(jnp.bfloat16)
            for n in range(4):
                rtx[n, us] = total[:, 16 * n : 16 * (n + 1)]
            for m in (1, 2, 3):
                r_copy(q, m).start()

        def step_c(q):
            t, c, k, us = where(q)
            pltpu.make_async_remote_copy(
                rrx.at[0:3, us], rrx.at[0:3, us], r_send.at[0], r_recv.at[q],
                device_id={"dp": partner}, device_id_type=ALONG).wait_recv()
            total = rtx[chip, us].astype(jnp.float32)
            for m in range(3):
                total = total + rrx[m, us].astype(jnp.float32)
            total = (total * (1.0 / (parts * tokens * act.shape[1] * shards))).astype(jnp.bfloat16)
            if t == 0:
                rrx[3, units(t, c)] = total
                f_copy(c, side).start()
            else:
                gathered[d, units(t, c)] = total
                spread(t, c)

        def step_d(q):
            t, c, k, us = where(q)
            if t == 1:
                relay(t, c)

        def drain():
            pltpu.make_async_remote_copy(
                give, prx, p_send.at[0], p_recv.at[0],
                device_id={"dp": partner}, device_id_type=ALONG).wait_send()
            for m in range(3):
                pltpu.make_async_remote_copy(
                    rtx.at[m], rrx.at[m], r_send.at[m], r_recv.at[0],
                    device_id={"dp": partner}, device_id_type=ALONG).wait_send()
            us = pl.ds(0, UNITS)
            pltpu.make_async_remote_copy(
                rrx.at[3, us], gathered.at[d, us], f_send.at[0], f_recv.at[0],
                device_id={"shard": side}, device_id_type=ALONG).wait_send()
            z_sent(out_way)

        steps = len(STEPS)
        for q in range(steps - 3):
            step_a(q, q - 2 if q >= 2 else None)
            step_b(q)
            if q >= 4:
                step_d(q - 4)
        e = steps - 3
        step_a(e, e - 2)
        step_a(e + 1)
        step_b(e)
        step_a(e + 2)
        step_b(e + 1)
        step_c(e - 1)
        step_b(e + 2)
        step_d(e - 4)
        step_d(e - 3)
        step_d(e - 2)
        step_c(e)
        step_c(e + 1)
        step_c(e + 2)
        step_d(e - 1)
        step_d(e)
        step_d(e + 1)
        drain()
        settle(0)
        step_d(e + 2)
        settle(1)
        finish()

    @pl.when(middle)
    def _():
        near = jnp.where(z == 1, 1, 0)
        far = 1 - near
        outward = jnp.where(z == 1, 0, last)
        loaded()

        def pass_g(way, n):
            g_copy(way, n).wait_recv()
            gtx[way, n, : ROWS[n]] = gsum(way, n)
            g_copy(way, n).start()

        def pass_s(way, k, h):
            s_copy(way, k, h).wait_recv()
            rows = slice(quarter * h, quarter * (h + 1))
            tx[way, k, rows] = (rx[way, k, rows].astype(jnp.float32) + tx[way, k, rows].astype(jnp.float32)).astype(jnp.bfloat16)
            s_copy(way, k, h).start()

        lag = CUTS + 1
        for n in range(GB):
            pass_g(near, n)
            if n >= lag:
                pass_g(far, n - lag)
        fill(near, 0)
        for h in range(CUTS):
            pass_s(near, 0, h)
            pass_g(far, GB - lag + h)
        fill(near, 1)
        fill(far, 0)
        pass_s(near, 1, 0)
        pass_g(far, GB - 1)
        for h in range(1, CUTS):
            pass_s(near, 1, h)
            pass_s(far, 0, h - 1)

        def both_ways(k, carry):
            fill(near, k)
            fill(far, k - 1)
            pass_s(near, k, 0)
            pass_s(far, k - 2, CUTS - 1)
            for h in range(1, CUTS):
                pass_s(near, k, h)
                pass_s(far, k - 1, h - 1)
            return carry

        lax.fori_loop(2, PIECES, both_ways, 0)
        fill(far, PIECES - 1)
        pass_s(far, PIECES - 2, CUTS - 1)
        for h in range(CUTS):
            pass_s(far, PIECES - 1, h)

        chunks = len(CHUNKS[0])
        for c in range(chunks):
            f_copy(c, outward).wait_recv()
            spread(0, c)
            if c >= 2:
                relay(0, c - 2)
        z_sent(near)
        z_sent(far)
        relay(0, chunks - 2)
        settle(0)
        relay(0, chunks - 1)
        settle(1)
        finish()


def assemble_kernel(source, out, got, held, sems):
    loads = []
    for i in range(COUNT):
        us = pl.ds(i * (i + 1) // 2, i + 1)
        loads.append(pltpu.make_async_copy(source.at[:, us], got.at[:, us], sems.at[COUNT + i]))
    for load in reversed(loads):
        load.start()
    half = BLK // 2

    def unit(u):
        rows = [got[2 * n + h, u] for h in range(2) for n in range(4)]
        return jnp.concatenate(rows, axis=0).astype(jnp.float32)

    def put(i):
        rows = pl.ds(BLK * i, BLK)
        return pltpu.make_async_copy(held.at[rows], out.at[rows], sems.at[i])

    final = COUNT - 1
    first = final * COUNT // 2
    lower = {}
    loads[final].wait()
    for v in range(COUNT // 2):
        top, bottom = unit(first + v), unit(first + COUNT // 2 + v)
        for g in range(2):
            rows = slice(half * g, half * (g + 1))
            lower[2 * v + g] = jnp.concatenate([top[rows], bottom[rows]], axis=0)
    square = lower[final]
    row = lax.broadcasted_iota(jnp.int32, (BLK, BLK), 0)
    col = lax.broadcasted_iota(jnp.int32, (BLK, BLK), 1)
    lower[final] = jnp.where((row < half) & (col >= half), square.T, square)
    for i in reversed(range(COUNT)):
        if i < final:
            loads[i].wait()
        for j in range(COUNT):
            if i == final:
                block = lower[j]
            elif j == final:
                block = lower[i].T
            elif j <= i:
                block = unit(i * (i + 1) // 2 + j)
            else:
                block = unit(j * (j + 1) // 2 + i).T
            held[BLK * i : BLK * (i + 1), BLK * j : BLK * (j + 1)] = block
        put(i).start()
    for i in range(COUNT):
        put(i).wait()


def fast_body(shards, parts, activations, out_grads, sign_bits, block_ids):
    tokens, columns = out_grads.shape
    per = columns // BLK
    own = block_ids.shape[1]
    hbm = pl.BlockSpec(memory_space=pltpu.HBM)
    bf, f32 = jnp.bfloat16, jnp.float32
    dma = pltpu.SemaphoreType.DMA
    steps, most = len(STEPS), len(CHUNKS[1])
    got = pl.pallas_call(
        functools.partial(mix_kernel, shards, parts, own, per),
        out_shape=jax.ShapeDtypeStruct((parts, UNITS, 16, BLK), bf),
        in_specs=[hbm, hbm, hbm, hbm],
        out_specs=hbm,
        scratch_shapes=[
            pltpu.VMEM(activations.shape, bf),
            pltpu.VMEM((per, tokens, BLK), bf),
            pltpu.VMEM(sign_bits.shape, jnp.int32),
            pltpu.VMEM((per, 1, BLK), f32),
            pltpu.SMEM(block_ids.shape, jnp.int32),
            pltpu.VMEM((2, PIECES, BLK, tokens), bf),
            pltpu.VMEM((2, PIECES, BLK, tokens), bf),
            pltpu.VMEM((2, GB, 128, 128), bf),
            pltpu.VMEM((2, GB, 128, 128), bf),
            pltpu.VMEM((tokens, tokens), f32),
            pltpu.VMEM((2, 128, 128), f32),
            pltpu.VMEM((16, 128), f32),
            pltpu.VMEM((tokens, tokens), bf),
            pltpu.VMEM((2, own * BLK, tokens), bf),
            pltpu.VMEM((2 * UNITS, 64, BLK), f32),
            pltpu.VMEM((2 * UNITS, 64, BLK), bf),
            pltpu.VMEM((2 * UNITS, 64, BLK), bf),
            pltpu.VMEM((4, 2 * UNITS, 16, BLK), bf),
            pltpu.VMEM((4, 2 * UNITS, 16, BLK), bf),
            pltpu.VMEM((parts, UNITS, 16, BLK), bf),
            dma((4,)), dma((2,)),
            dma((2, 3)), dma((2, GB + CUTS * PIECES)),
            dma((1,)), dma((steps,)),
            dma((3,)), dma((steps,)),
            dma((1,)), dma((COUNT,)),
            dma((4,)), dma((most + 2,)),
            dma((1,)), dma((2,)),
        ],
        compiler_params=pltpu.CompilerParams(collective_id=0, has_side_effects=True, vmem_limit_bytes=int(62.5 * 2**20)),
        name="mix",
    )(activations, out_grads, sign_bits, block_ids)
    return pl.pallas_call(
        assemble_kernel,
        out_shape=jax.ShapeDtypeStruct((own * BLK, own * BLK), f32),
        in_specs=[hbm],
        out_specs=hbm,
        scratch_shapes=[
            pltpu.VMEM((parts, UNITS, 16, BLK), bf), pltpu.VMEM((own * BLK, own * BLK), f32), dma((2 * own,))],
        compiler_params=pltpu.CompilerParams(vmem_limit_bytes=int(62.5 * 2**20)),
        name="assemble",
    )(got)


def solution(mesh):
    in_specs = (P("dp", "shard"), P("dp", "shard"), P("shard"), P())
    out_specs = P("shard", None)
    shards, parts = mesh.shape["shard"], mesh.shape["dp"]
    chosen = functools.partial(fast_body, shards, parts) if (shards, parts) == (4, 8) else body
    return jax.shard_map(chosen, mesh=mesh, in_specs=in_specs, out_specs=out_specs, check_vma=False)
```
